32 devices in a mesh: dp: 16 (over z, y, x), mp: 2 (over core).
Axes of the slice: x: 2, y: 2, z: 4, core: 2. Of those that a mesh axis runs over, the one named last changes fastest.
Arguments:
- history: bfloat16 [4, 2048, 2048], P(None, 'dp'), may hold values from -6 to 6
- cotangent: bfloat16 [2048, 2048], P('dp'), may hold values from -6 to 6
- weight_query: bfloat16 [2048, 2048], P('dp', 'mp'), may hold values from -0.125 to 0.125
- weight_key: bfloat16 [2048, 2048], P('dp', 'mp'), may hold values from -0.125 to 0.125
- weight_value: bfloat16 [2048, 2048], P('dp', 'mp'), may hold values from -0.125 to 0.125
- weight_out: bfloat16 [2048, 2048], P('mp', 'dp'), may hold values from -0.5 to 0.5
- weight_up: bfloat16 [2048, 8192], P('dp', 'mp'), may hold values from -0.125 to 0.125
- weight_down: bfloat16 [8192, 2048], P('mp', 'dp'), may hold values from -0.0625 to 0.0625
- bias_query: bfloat16 [2048], P('mp'), may hold values from -3 to 3
- bias_key: bfloat16 [2048], P('mp'), may hold values from -3 to 3
- bias_value: bfloat16 [2048], P('mp'), may hold values from -3 to 3
- out_bias: bfloat16 [2048], replicated, may hold values from -3 to 3
- bias_up: bfloat16 [8192], P('mp'), may hold values from -3 to 3
- attn_gain: bfloat16 [2048], replicated, may hold values from 0.5 to 1.5
- attn_shift: bfloat16 [2048], replicated, may hold values from -3 to 3
- mlp_gain: bfloat16 [2048], replicated, may hold values from 0.5 to 1.5
- mlp_shift: bfloat16 [2048], replicated, may hold values from -3 to 3
- mix_gain: bfloat16 [2048], replicated, may hold values from 0.5 to 1.5
- mix_in: bfloat16 [2048, 68], replicated, may hold values from -0.125 to 0.125
- mix_out: bfloat16 [68, 16], replicated, may hold values from -0.75 to 0.75
- mix_bias: bfloat16 [16], replicated, may hold values from -4 to 4
Outputs:
- block_out: bfloat16 [2048, 2048], P('dp')
- grad_history: float32 [4, 2048, 2048], P(None, ('dp', 'mp'))
- grad_weight_query: float32 [2048, 2048], P('dp', 'mp')
- grad_weight_key: float32 [2048, 2048], P('dp', 'mp')
- grad_weight_value: float32 [2048, 2048], P('dp', 'mp')
- grad_weight_out: float32 [2048, 2048], P('mp', 'dp')
- grad_weight_up: float32 [2048, 8192], P('dp', 'mp')
- grad_weight_down: float32 [8192, 2048], P('mp', 'dp')
- grad_bias_query: float32 [2048], replicated
- grad_bias_key: float32 [2048], replicated
- grad_bias_value: float32 [2048], replicated
- grad_out_bias: float32 [2048], replicated
- grad_bias_up: float32 [8192], replicated
- grad_attn_gain: float32 [2048], replicated
- grad_attn_shift: float32 [2048], replicated
- grad_mlp_gain: float32 [2048], replicated
- grad_mlp_shift: float32 [2048], replicated
- grad_mix_gain: float32 [2048], replicated
- grad_mix_in: float32 [2048, 68], replicated
- grad_mix_out: float32 [68, 16], replicated
- grad_mix_bias: float32 [16], replicated
- mix_stats: float32 [2, 16], replicated
The draws below stay inside these ranges and needn't reach their ends.
All inputs are finite; a program needn't handle non-finite values.
Results may differ from the reference program's by a relative error of at most 0.02.
The reference program's roundings to bfloat16 on the way count: a program that leaves them out, or rounds other values in their place, can miss the bound.
Values may be sent and summed in bfloat16 or wider, within the bound.
No kernel may reach another device: no remote copies, remote signals or barrier semaphores. Data moves between devices by JAX's collectives and lax.ppermute only.
A program may use at most 256 MiB of HBM per device.

```python
import math
import jax
import jax.numpy as jnp
from jax import lax

D = 2048
HEADS = 16
HEAD_DIM = 128
FF = 8192
ROT = 32
MIX_HID = 68
NH = 4
SEQ_LEN = 128
TOKENS = 2048
N_DP = 16


def with_spikes(array, own_key, source, target, parts, factor):
    def block_of(dim):
        return (jnp.arange(array.shape[dim]) // (array.shape[dim] // parts)).reshape((-1,) + (1,) * (array.ndim - 1 - dim))

    first = jax.random.permutation(own_key, parts)[block_of(target)]
    other_side = (block_of(target) + parts // 2) % parts
    return jnp.where((block_of(source) == first) | (block_of(source) == other_side), factor * array, array)


def steps_of(stream_key, dims, pieces, smallest, top_value):
    level, own = 1.0, jax.random.fold_in(stream_key, 6)
    for position, parts in pieces:
        steps = jnp.exp(jax.random.uniform(jax.random.fold_in(own, position), (parts,), jnp.float32, smallest / len(pieces), top_value / len(pieces)))
        level = level * jnp.repeat(steps, dims[position] // parts).reshape([-1 if axis == position else 1 for axis in range(len(dims))])
    return level


def scatter_about(key, shape, width, bound, split=(), kind=jnp.bfloat16):
    factor_of = steps_of(key, shape, split, -0.22, 0.18) if split else 1.0
    drawn = jax.random.normal(key, shape, jnp.float32) * width * factor_of
    return jnp.minimum(jnp.maximum(drawn, -bound), bound).astype(kind)


def gaussian_with(own_key, dims, spread, bound, pieces, heavy, kind=jnp.bfloat16):
    drawn = spread * jax.random.normal(own_key, dims, jnp.float32)
    if pieces:
        drawn = drawn * steps_of(own_key, dims, pieces, -0.22, 0.18)
    return jnp.clip(with_spikes(drawn, jax.random.fold_in(own_key, 3), *heavy), -bound, bound).astype(kind)


def setup_inputs(seed: int = 0) -> dict:
    streams_of = jax.random.split(jax.random.key(seed), 22)
    return {
        "history": scatter_about(streams_of[0], (NH, TOKENS, D), 1.0, 6.0, ((1, 16),)),
        "cotangent": gaussian_with(streams_of[1], (TOKENS, D), 1.0, 6.0, ((0, 16),), (0, 1, 16, 2.0)),
        "weight_query": scatter_about(streams_of[2], (D, D), D ** -0.5, 0.125, ((0, 16), (1, 2))),
        "weight_key": scatter_about(streams_of[3], (D, D), D ** -0.5, 0.125, ((0, 16), (1, 2))),
        "weight_value": scatter_about(streams_of[4], (D, D), D ** -0.5, 0.125, ((0, 16), (1, 2))),
        "weight_out": scatter_about(streams_of[5], (D, D), (D // 16) ** -0.5, 0.5, ((0, 2), (1, 16))),
        "weight_up": scatter_about(streams_of[6], (D, FF), D ** -0.5, 0.125, ((0, 16), (1, 2))),
        "weight_down": scatter_about(streams_of[7], (FF, D), FF ** -0.5, 0.0625, ((0, 2), (1, 16))),
        "bias_query": scatter_about(streams_of[8], (D,), 0.5, 3.0, ((0, 2),)),
        "bias_key": scatter_about(streams_of[9], (D,), 0.5, 3.0, ((0, 2),)),
        "bias_value": scatter_about(streams_of[10], (D,), 0.5, 3.0, ((0, 2),)),
        "out_bias": scatter_about(streams_of[11], (D,), 0.5, 3.0),
        "bias_up": scatter_about(streams_of[12], (FF,), 0.5, 3.0, ((0, 2),)),
        "attn_gain": jnp.clip(1.0 + 0.1 * jax.random.normal(streams_of[13], (D,), jnp.float32), 0.5, 1.5).astype(jnp.bfloat16),
        "attn_shift": scatter_about(streams_of[14], (D,), 0.5, 3.0),
        "mlp_gain": jnp.clip(1.0 + 0.1 * jax.random.normal(streams_of[15], (D,), jnp.float32), 0.5, 1.5).astype(jnp.bfloat16),
        "mlp_shift": scatter_about(streams_of[16], (D,), 0.5, 3.0),
        "mix_gain": jnp.clip(1.0 + 0.1 * jax.random.normal(streams_of[17], (D,), jnp.float32), 0.5, 1.5).astype(jnp.bfloat16),
        "mix_in": scatter_about(streams_of[18], (D, MIX_HID), D ** -0.5, 0.125),
        "mix_out": scatter_about(streams_of[19], (MIX_HID, 4 * NH), MIX_HID ** -0.5, 0.75),
        "mix_bias": scatter_about(streams_of[20], (4 * NH,), 1.0, 4.0),
    }


EPS = 1e-05
HIGH = lax.Precision.HIGHEST

@jax.custom_vjp
def low(v):
    return lax.optimization_barrier(v.astype(jnp.bfloat16)).astype(jnp.float32)

@jax.custom_vjp
def low_back(v):
    return v

def low_keep(v):
    return (low(v), None)

def low_pass(kept, grad):
    return (grad,)

def back_keep(v):
    return (v, None)

def back_low(kept, grad):
    return (low(grad),)
low.defvjp(low_keep, low_pass)
low_back.defvjp(back_keep, back_low)

def layer_norm(values, gain, shift):
    center = values - lax.optimization_barrier(jnp.mean(values, -1, keepdims=True))
    return center * lax.rsqrt(lax.optimization_barrier(jnp.mean(center * center, -1, keepdims=True)) + EPS) * gain + shift

def angle_tables(length):
    half_rot = ROT // 2
    frequency = jnp.exp(jnp.arange(half_rot, dtype=jnp.float32) * (-2.0 * math.log(10000.0) / ROT))
    angles = jnp.arange(length, dtype=jnp.float32)[:, None] * frequency[None, :]
    return (jnp.cos(angles), jnp.sin(angles))

def rotate(values, cosine, sine_table):
    half_rot = ROT // 2
    first_part = values[..., :half_rot]
    second_part = values[..., half_rot:ROT]
    cos_heads = cosine[:, None, :]
    sin_heads = sine_table[:, None, :]
    return jnp.concatenate([first_part * cos_heads - second_part * sin_heads, second_part * cos_heads + first_part * sin_heads, values[..., ROT:]], -1)

def forward(params, hist_seq):
    weight_query, weight_key, weight_value, weight_out, weight_up, weight_down, bias_query, bias_key, bias_value, out_bias, bias_up, attn_gain, attn_shift, mlp_gain, mlp_shift, mix_gain, mix_in, mix_out, mix_bias = params
    length = hist_seq.shape[1]
    last_out = hist_seq[NH - 1]
    zed = low(last_out * lax.rsqrt(lax.optimization_barrier(jnp.mean(last_out * last_out, -1, keepdims=True)) + EPS) * mix_gain)
    mix_pre = low_back(jnp.dot(zed, mix_in, precision=HIGH))
    mix_act = low(jax.nn.gelu(mix_pre, approximate=False))
    mix_weights = low_back(jnp.dot(mix_act, mix_out, precision=HIGH) + mix_bias)
    mix_grid = mix_weights.reshape(length, 4, NH)
    streams = jnp.einsum('scj,jsd->csd', mix_grid, hist_seq, precision=HIGH)
    in_query = low(layer_norm(streams[0], attn_gain, attn_shift))
    in_key = low(layer_norm(streams[1], attn_gain, attn_shift))
    in_value = low(layer_norm(streams[2], attn_gain, attn_shift))
    q_pre = low_back(jnp.dot(in_query, weight_query, precision=HIGH) + bias_query)
    k_pre = low_back(jnp.dot(in_key, weight_key, precision=HIGH) + bias_key)
    values = low(low_back(jnp.dot(in_value, weight_value, precision=HIGH) + bias_value)).reshape(length, HEADS, HEAD_DIM)
    cosine, sine_table = angle_tables(length)
    queries = low(rotate(q_pre.reshape(length, HEADS, HEAD_DIM), cosine, sine_table))
    keys = low(rotate(k_pre.reshape(length, HEADS, HEAD_DIM), cosine, sine_table))
    raw_scores = low_back(jnp.einsum('qhd,khd->hqk', queries, keys, precision=HIGH) * HEAD_DIM ** (-0.5))
    positions = jnp.arange(length)
    causal = positions[:, None] >= positions[None, :]
    scores = jnp.where(causal[None], raw_scores, -1e+30)
    attn_probs = jax.nn.softmax(scores, axis=-1)
    mixed = jnp.einsum('hqk,khd->qhd', low(attn_probs), values, precision=HIGH).reshape(length, HEADS * HEAD_DIM)
    mixed = low(low_back(mixed))
    attn_part = jnp.dot(mixed, weight_out, precision=HIGH)
    in_resid = low(layer_norm(streams[3], mlp_gain, mlp_shift))
    up_pre = low_back(jnp.dot(in_resid, weight_up, precision=HIGH) + bias_up)
    gelu_out = low(jax.nn.gelu(up_pre, approximate=False))
    mlp_part = jnp.dot(gelu_out, weight_down, precision=HIGH)
    return (streams[3] + attn_part + mlp_part + out_bias, mix_weights)

def reference(history, cotangent, weight_query, weight_key, weight_value, weight_out, weight_up, weight_down, bias_query, bias_key, bias_value, out_bias, bias_up, attn_gain, attn_shift, mlp_gain, mlp_shift, mix_gain, mix_in, mix_out, mix_bias):
    params = tuple((member.astype(jnp.float32) for member in (weight_query, weight_key, weight_value, weight_out, weight_up, weight_down, bias_query, bias_key, bias_value, out_bias, bias_up, attn_gain, attn_shift, mlp_gain, mlp_shift, mix_gain, mix_in, mix_out, mix_bias)))
    hist_seqs = history.astype(jnp.float32).reshape(NH, N_DP, SEQ_LEN, D).transpose(1, 0, 2, 3)
    cot_seqs = cotangent.astype(jnp.float32).reshape(N_DP, SEQ_LEN, D)

    def one_seq(totals, inputs):
        hist_seq, cot_seq = inputs
        out_seq, pull_back, mix_weights = jax.vjp(forward, params, hist_seq, has_aux=True)
        grad_params, grad_hist = pull_back(cot_seq)
        return (jax.tree.map(jnp.add, totals, grad_params), (out_seq, grad_hist, mix_weights))
    totals, (out_seqs, grad_hists, mix_all) = lax.scan(one_seq, jax.tree.map(jnp.zeros_like, params), (hist_seqs, cot_seqs))
    flat_weights = mix_all.reshape(TOKENS, 4 * NH)
    mean_weights = lax.optimization_barrier(jnp.mean(flat_weights, 0))
    var_weights = lax.optimization_barrier(jnp.mean(flat_weights * flat_weights, 0)) - mean_weights * mean_weights
    return (out_seqs.reshape(TOKENS, D).astype(jnp.bfloat16), grad_hists.transpose(1, 0, 2, 3).reshape(NH, TOKENS, D), totals[0], totals[1], totals[2], totals[3], totals[4], totals[5], totals[6], totals[7], totals[8], totals[9], totals[10], totals[11], totals[12], totals[13], totals[14], totals[15], totals[16], totals[17], totals[18], jnp.stack([mean_weights, var_weights]))
```

```python
import math

import jax
import jax.numpy as jnp
from jax import lax
from jax.sharding import Mesh, PartitionSpec as P

HEAD_DIM = 128
ROT = 32
EPS = 1e-05
NB = 4
SWAP = ((0, 1), (1, 0))
F32 = jnp.float32
BF16 = jnp.bfloat16


def contract(left, right, left_dim, right_dim):
    return lax.dot_general(
        left, right, (((left_dim,), (right_dim,)), ((), ())), preferred_element_type=F32
    )


def norm_parts(values):
    center = values - jnp.mean(values, -1, keepdims=True)
    inverse = lax.rsqrt(jnp.mean(center * center, -1, keepdims=True) + EPS)
    return center * inverse, inverse


def norm_back(grad_out, normed, inverse, gain):
    scaled = grad_out * gain
    return inverse * (
        scaled
        - jnp.mean(scaled, -1, keepdims=True)
        - normed * jnp.mean(scaled * normed, -1, keepdims=True)
    )


def phi_parts(values):
    cdf = 0.5 * (1.0 + lax.erf(values * (1.0 / math.sqrt(2.0))))
    pdf = jnp.exp(-0.5 * values * values) * (1.0 / math.sqrt(2.0 * math.pi))
    return cdf, pdf


def rotate(values, cosine, sine_table):
    half_rot = ROT // 2
    first_part = values[..., :half_rot]
    second_part = values[..., half_rot:ROT]
    return jnp.concatenate(
        [
            first_part * cosine - second_part * sine_table,
            second_part * cosine + first_part * sine_table,
            values[..., ROT:],
        ],
        -1,
    )


def ring(values):
    size = lax.axis_size("b")
    return lax.ppermute(values, "b", [(i, (i + 1) % size) for i in range(size)])


def swap_core(values):
    return lax.ppermute(values, "mp", SWAP)


def to_gathered(values):
    rows, width = values.shape
    nb, na = lax.axis_size("b"), lax.axis_size("a")
    return values.reshape(rows, nb, na, width // (nb * na)).transpose(0, 2, 1, 3).reshape(rows, width)


def from_gathered(values):
    rows, width = values.shape
    nb, na = lax.axis_size("b"), lax.axis_size("a")
    return values.reshape(rows, na, nb, width // (nb * na)).transpose(0, 2, 1, 3).reshape(rows, width)


def gather_tokens(values):
    slots = [values]
    for _ in range(lax.axis_size("b") - 1):
        slots.append(ring(slots[-1]))
    mine = jnp.stack(slots, -3)
    return jnp.stack([mine, swap_core(mine)], -3)


def scatter_tokens(part):
    other = swap_core(part[:, 1].astype(BF16))
    pair = part[:, 0] + other.astype(F32)
    moving = pair[1].astype(BF16)
    size = lax.axis_size("b")
    for step in range(2, size):
        moving = (ring(moving).astype(F32) + pair[step]).astype(BF16)
    return ring(moving).astype(F32) + pair[0]


def exchange_b(values):
    return lax.all_to_all(values, "b", 0, 0, tiled=True)


def weights_cols(weight):
    rows, cols = weight.shape
    nb = lax.axis_size("b")
    blocks = weight.reshape(rows, nb, cols // nb).transpose(1, 0, 2)
    full = lax.all_gather(exchange_b(blocks), "a", axis=0, tiled=True)
    return full.reshape(-1, cols // nb)


def weights_rows(weight):
    rows, cols = weight.shape
    nb = lax.axis_size("b")
    blocks = weight.reshape(nb, rows // nb, cols)
    full = lax.all_gather(exchange_b(blocks), "a", axis=0, tiled=True)
    return full.transpose(1, 0, 2).reshape(rows // nb, -1)


def grads_cols(grad):
    nb, na = lax.axis_size("b"), lax.axis_size("a")
    blocks = grad.astype(BF16).reshape(na * nb, grad.shape[0] // (na * nb), grad.shape[1])
    mine = lax.psum_scatter(blocks, "a", scatter_dimension=0, tiled=True)
    return exchange_b(mine).astype(F32).transpose(1, 0, 2)


def grads_rows(grad):
    nb, na = lax.axis_size("b"), lax.axis_size("a")
    rows = grad.shape[0]
    blocks = grad.astype(BF16).reshape(rows, na * nb, grad.shape[1] // (na * nb)).transpose(1, 0, 2)
    mine = lax.psum_scatter(blocks, "a", scatter_dimension=0, tiled=True)
    return exchange_b(mine).astype(F32).reshape(nb * rows, -1)


def sum_small(items):
    axes = ("b", "a", "mp")
    count = lax.axis_size(axes)
    flat = jnp.concatenate([item.reshape(-1) for item in items])
    size = flat.shape[0]
    unit = count * 1024
    padded = -(-size // unit) * unit
    flat = jnp.pad(flat, (0, padded - size)).reshape(count, -1, 128)
    mine = jnp.sum(lax.all_to_all(flat, axes, 0, 0, tiled=True), 0)
    full = lax.all_gather(mine, axes, axis=0, tiled=True).reshape(-1)
    out, at = [], 0
    for item in items:
        out.append(full[at : at + item.size].reshape(item.shape))
        at += item.size
    return out


def place(values, full_len, index):
    return lax.dynamic_update_slice_in_dim(
        jnp.zeros((full_len,), F32), values, index * values.shape[0], 0
    )


def shards(
    history,
    cotangent,
    weight_query,
    weight_key,
    weight_value,
    weight_out,
    weight_up,
    weight_down,
    bias_query,
    bias_key,
    bias_value,
    out_bias,
    bias_up,
    attn_gain,
    attn_shift,
    mlp_gain,
    mlp_shift,
    mix_gain,
    mix_in,
    mix_out,
    mix_bias,
):
    entries, length, width = history.shape
    nb = lax.axis_size("b")
    n_mp = lax.axis_size("mp")
    core = lax.axis_index("mp")
    line = lax.axis_index("b")
    half = length // n_mp
    start = core * half

    cot = lax.dynamic_slice_in_dim(cotangent, start, half, 0)
    full_cot = gather_tokens(to_gathered(cot)).reshape(-1, width)

    hist = lax.dynamic_slice_in_dim(history, start, half, 1).astype(F32)
    last = hist[entries - 1]
    rms_inverse = lax.rsqrt(jnp.mean(last * last, -1, keepdims=True) + EPS)
    mix_gain_f = mix_gain.astype(F32)
    zed = (last * rms_inverse * mix_gain_f).astype(BF16)
    mix_pre = jnp.dot(zed, mix_in, preferred_element_type=F32)
    mix_cdf, mix_pdf = phi_parts(mix_pre)
    mix_act = (mix_pre * mix_cdf).astype(BF16)
    mix_weights = jnp.dot(mix_act, mix_out, preferred_element_type=F32) + mix_bias.astype(F32)
    grid = mix_weights.reshape(half, 4, entries)
    streams = []
    for stream in range(4):
        total = grid[:, stream, 0, None] * hist[0]
        for source in range(1, entries):
            total = total + grid[:, stream, source, None] * hist[source]
        streams.append(total)
    attn_gain_f, attn_shift_f = attn_gain.astype(F32), attn_shift.astype(F32)
    mlp_gain_f, mlp_shift_f = mlp_gain.astype(F32), mlp_shift.astype(F32)
    gains = (attn_gain_f, attn_gain_f, attn_gain_f, mlp_gain_f)
    shifts = (attn_shift_f, attn_shift_f, attn_shift_f, mlp_shift_f)
    norms = [norm_parts(value) for value in streams]
    inputs = [
        to_gathered((norm[0] * gain + shift).astype(BF16))
        for norm, gain, shift in zip(norms, gains, shifts)
    ]

    full_up = weights_cols(weight_up)
    in_resid = gather_tokens(inputs[3]).reshape(-1, width)
    full_down = weights_rows(weight_down)
    hidden = full_up.shape[1]
    bias_up_mine = lax.dynamic_slice_in_dim(bias_up, line * hidden, hidden, 0).astype(F32)
    up_pre = jnp.dot(in_resid, full_up, preferred_element_type=F32) + bias_up_mine
    cdf, pdf = phi_parts(up_pre)
    gelu_out = (up_pre * cdf).astype(BF16)
    grad_gelu = contract(full_cot, full_down, 1, 1)
    grad_up = (grad_gelu * (cdf + up_pre * pdf)).astype(BF16)
    grad_up_full = contract(in_resid, grad_up, 0, 0)
    grad_down_full = contract(gelu_out, full_cot, 0, 0)
    part_resid = contract(grad_up, full_up, 1, 1)
    mlp_part = jnp.dot(gelu_out, full_down, preferred_element_type=F32)
    grad_bias_up = jnp.sum(grad_up.astype(F32), 0)

    qkv = jnp.stack([weight_query, weight_key, weight_value], 1)
    rows = weight_query.shape[0]
    qkv = qkv.reshape(rows, 3, nb, -1).transpose(0, 2, 1, 3).reshape(rows, -1)
    full_qkv = weights_cols(qkv)
    head_cols = full_qkv.shape[1] // 3
    heads = head_cols // HEAD_DIM
    full_out = weights_rows(weight_out)
    in_qkv = gather_tokens(jnp.stack(inputs[:3])).reshape(3, -1, width)
    pre = []
    for stream, bias in enumerate((bias_query, bias_key, bias_value)):
        mine = lax.dynamic_slice_in_dim(bias, line * head_cols, head_cols, 0).astype(F32)
        full = full_qkv[:, stream * head_cols : (stream + 1) * head_cols]
        pre.append(jnp.dot(in_qkv[stream], full, preferred_element_type=F32) + mine)
    half_rot = ROT // 2
    frequency = jnp.exp(jnp.arange(half_rot, dtype=F32) * (-2.0 * math.log(10000.0) / ROT))
    positions = (jnp.arange(length) + start) % length
    angles = positions.astype(F32)[:, None] * frequency[None, :]
    cosine = jnp.cos(angles)[None, :, None, :]
    sine = jnp.sin(angles)[None, :, None, :]
    split = lambda value: value.reshape(nb, length, heads, HEAD_DIM)
    queries = rotate(split(pre[0]), cosine, sine).astype(BF16)
    keys = rotate(split(pre[1]), cosine, sine).astype(BF16)
    values = split(pre[2]).astype(BF16)
    causal = positions[:, None] >= positions[None, :]
    scale = HEAD_DIM ** (-0.5)
    scores = jnp.einsum("sqhd,skhd->shqk", queries, keys, preferred_element_type=F32) * scale
    scores = jnp.where(causal, scores, -1e30)
    expon = jnp.exp(scores - jnp.max(scores, -1, keepdims=True))
    probs = expon / jnp.sum(expon, -1, keepdims=True)
    probs_low = probs.astype(BF16)
    mixed = jnp.einsum("shqk,skhd->sqhd", probs_low, values, preferred_element_type=F32)
    mixed = mixed.reshape(nb * length, head_cols).astype(BF16)
    branch = mlp_part + jnp.dot(mixed, full_out, preferred_element_type=F32)
    grad_out_full = contract(mixed, full_cot, 0, 0)
    grad_heads = split(contract(full_cot, full_out, 1, 1).astype(BF16))
    grad_values = jnp.einsum("shqk,sqhd->skhd", probs_low, grad_heads, preferred_element_type=F32)
    grad_probs = jnp.einsum("sqhd,skhd->shqk", grad_heads, values, preferred_element_type=F32)
    row_delta = jnp.sum(probs * grad_probs, -1, keepdims=True)
    grad_scores = (probs * (grad_probs - row_delta)).astype(BF16)
    grad_queries = jnp.einsum("shqk,skhd->sqhd", grad_scores, keys, preferred_element_type=F32)
    grad_keys = jnp.einsum("shqk,sqhd->skhd", grad_scores, queries, preferred_element_type=F32)
    flat = lambda value: value.reshape(nb * length, head_cols).astype(BF16)
    grad_pre = (
        flat(rotate(grad_queries * scale, cosine, -sine)),
        flat(rotate(grad_keys * scale, cosine, -sine)),
        flat(grad_values),
    )
    grad_qkv_full = jnp.concatenate(
        [contract(in_qkv[stream], grad_pre[stream], 0, 0) for stream in range(3)], 1
    )
    grad_bias_qkv = [jnp.sum(value.astype(F32), 0) for value in grad_pre]
    parts = [
        contract(grad_pre[stream], full_qkv[:, stream * head_cols : (stream + 1) * head_cols], 1, 1)
        for stream in range(3)
    ]
    parts.append(part_resid)

    shape = (nb, n_mp, half, width)
    branch_mine = from_gathered(scatter_tokens(branch.reshape(shape)))
    incoming = [from_gathered(scatter_tokens(part.reshape(shape))) for part in parts]
    block_half = (streams[3] + branch_mine + out_bias.astype(F32)).astype(BF16)
    block_other = swap_core(block_half)
    first = core == 0
    block_out = jnp.concatenate(
        [jnp.where(first, block_half, block_other), jnp.where(first, block_other, block_half)], 0
    )

    cot_f = cot.astype(F32)
    stream_grads = [
        norm_back(grad, norm[0], norm[1], gain) for grad, norm, gain in zip(incoming, norms, gains)
    ]
    stream_grads[3] = stream_grads[3] + cot_f
    grad_attn_gain = jnp.sum(sum(incoming[c] * norms[c][0] for c in range(3)), 0)
    grad_attn_shift = jnp.sum(sum(incoming[c] for c in range(3)), 0)
    grad_mlp_gain = jnp.sum(incoming[3] * norms[3][0], 0)
    grad_mlp_shift = jnp.sum(incoming[3], 0)
    cells = [
        jnp.sum(stream_grads[stream] * hist[source], -1)
        for stream in range(4)
        for source in range(entries)
    ]
    grad_mix_low = jnp.stack(cells, -1).astype(BF16)
    grad_hist = []
    for source in range(entries):
        total = grid[:, 0, source, None] * stream_grads[0]
        for stream in range(1, 4):
            total = total + grid[:, stream, source, None] * stream_grads[stream]
        grad_hist.append(total)
    grad_mix_bias = jnp.sum(grad_mix_low.astype(F32), 0)
    grad_mix_out = contract(mix_act, grad_mix_low, 0, 0)
    grad_mix_act = contract(grad_mix_low, mix_out, 1, 1)
    grad_mix_pre = (grad_mix_act * (mix_cdf + mix_pre * mix_pdf)).astype(BF16)
    grad_mix_in = contract(zed, grad_mix_pre, 0, 0)
    grad_zed = contract(grad_mix_pre, mix_in, 1, 1)
    last_normed = last * rms_inverse
    grad_mix_gain = jnp.sum(grad_zed * last_normed, 0)
    zed_scaled = grad_zed * mix_gain_f
    grad_last = rms_inverse * (
        zed_scaled - last_normed * jnp.mean(zed_scaled * last_normed, -1, keepdims=True)
    )
    grad_hist[entries - 1] = grad_hist[entries - 1] + grad_last
    grad_history = jnp.stack(grad_hist, 0)

    up_shard = grads_cols(grad_up_full).reshape(rows, -1)
    down_shard = grads_rows(grad_down_full)
    qkv_shard = grads_cols(grad_qkv_full).reshape(rows, nb, 3, head_cols)
    query_shard, key_shard, value_shard = (
        qkv_shard[:, :, stream].reshape(rows, -1) for stream in range(3)
    )
    out_shard = grads_rows(grad_out_full)

    block = core * nb + line
    (
        grad_bias_up,
        grad_bias_query,
        grad_bias_key,
        grad_bias_value,
        grad_out_bias,
        grad_attn_gain,
        grad_attn_shift,
        grad_mlp_gain,
        grad_mlp_shift,
        grad_mix_gain,
        grad_mix_in,
        grad_mix_out,
        grad_mix_bias,
        stat_first,
        stat_second,
    ) = sum_small(
        [
            place(grad_bias_up, bias_up.shape[0] * n_mp, block),
            *(place(value, width, block) for value in grad_bias_qkv),
            jnp.sum(cot_f, 0),
            grad_attn_gain,
            grad_attn_shift,
            grad_mlp_gain,
            grad_mlp_shift,
            grad_mix_gain,
            grad_mix_in,
            grad_mix_out,
            grad_mix_bias,
            jnp.sum(mix_weights, 0),
            jnp.sum(mix_weights * mix_weights, 0),
        ]
    )
    tokens = length * nb * lax.axis_size("a")
    mean_weights = stat_first / tokens
    var_weights = stat_second / tokens - mean_weights * mean_weights
    mix_stats = jnp.stack([mean_weights, var_weights])
    return (
        block_out,
        grad_history,
        query_shard,
        key_shard,
        value_shard,
        out_shard,
        up_shard,
        down_shard,
        grad_bias_query,
        grad_bias_key,
        grad_bias_value,
        grad_out_bias,
        grad_bias_up,
        grad_attn_gain,
        grad_attn_shift,
        grad_mlp_gain,
        grad_mlp_shift,
        grad_mix_gain,
        grad_mix_in,
        grad_mix_out,
        grad_mix_bias,
        mix_stats,
    )


def solution(mesh):
    n_dp, n_mp = mesh.shape["dp"], mesh.shape["mp"]
    fine = Mesh(mesh.devices.reshape(NB, n_dp // NB, n_mp), ("b", "a", "mp"))
    dp = ("b", "a")
    whole = P()
    in_specs = (
        P(None, dp, None),
        P(dp, None),
        P(dp, "mp"),
        P(dp, "mp"),
        P(dp, "mp"),
        P("mp", dp),
        P(dp, "mp"),
        P("mp", dp),
        P("mp"),
        P("mp"),
        P("mp"),
        whole,
        P("mp"),
    ) + (whole,) * 8
    out_specs = (
        P(dp, None),
        P(None, dp + ("mp",), None),
        P(dp, "mp"),
        P(dp, "mp"),
        P(dp, "mp"),
        P("mp", dp),
        P(dp, "mp"),
        P("mp", dp),
    ) + (whole,) * 14
    return jax.shard_map(shards, mesh=fine, in_specs=in_specs, out_specs=out_specs, check_vma=False)
```

```python
import functools
import math

import jax
import jax.numpy as jnp
import numpy as np
from jax import lax
from jax.experimental import pallas as pl
from jax.experimental.pallas import tpu as pltpu
from jax.sharding import Mesh, PartitionSpec as P


HEAD_DIM = 128
ROT = 32
EPS = 1e-05
NB = 4
LANES = 128
CHUNK = 16
SWAP = ((0, 1), (1, 0))
F32 = jnp.float32
BF16 = jnp.bfloat16
NN, NT, TN = ((1,), (0,)), ((1,), (1,)), ((0,), (0,))


def mm(left, right, dims=NN):
    return lax.dot_general(left, right, (dims, ((), ())), preferred_element_type=F32)


def norm_parts(values):
    center = values - jnp.mean(values, -1, keepdims=True)
    inverse = lax.rsqrt(jnp.mean(center * center, -1, keepdims=True) + EPS)
    return center * inverse, inverse


def norm_back(grad_out, normed, inverse, gain):
    scaled = grad_out * gain
    return inverse * (
        scaled
        - jnp.mean(scaled, -1, keepdims=True)
        - normed * jnp.mean(scaled * normed, -1, keepdims=True)
    )


def phi_parts(values):
    cdf = 0.5 * (1.0 + lax.erf(values * (1.0 / math.sqrt(2.0))))
    pdf = jnp.exp(-0.5 * values * values) * (1.0 / math.sqrt(2.0 * math.pi))
    return cdf, pdf


def lane_blocks(width, nb, na):
    size = width // (nb * na)
    return [
        (slice((b * na + a) * size, (b * na + a + 1) * size), (a * nb + b) * size, size)
        for a in range(na)
        for b in range(nb)
    ]


def from_gathered(values, nb, na):
    blocks = sorted(lane_blocks(values.shape[-1], nb, na), key=lambda item: item[0].start)
    return jnp.concatenate([values[:, at : at + size] for _, at, size in blocks], -1)


def mix_rows(hist, weights, stream):
    entries = len(hist)
    total = weights[:, stream * entries : stream * entries + 1] * hist[0]
    for source in range(1, entries):
        at = stream * entries + source
        total = total + weights[:, at : at + 1] * hist[source]
    return total


def local_forward_body(
    nb, na, core, hist, cot, vecs, mix_in, mix_out, mix_bias, qkv, resid, cot_out, weights, pre, zed
):
    entries, half, width = hist.shape
    del core

    def first(step, _):
        rows = pl.ds(pl.multiple_of(step * CHUNK, CHUNK), CHUNK)
        last = hist[entries - 1, rows, :].astype(F32)
        inverse = lax.rsqrt(jnp.mean(last * last, -1, keepdims=True) + EPS)
        zed[rows, :] = (last * inverse * vecs[4:5, :]).astype(BF16)
        value = cot[rows, :]
        for source, at, size in lane_blocks(width, nb, na):
            cot_out[rows, at : at + size] = value[:, source]
        return 0

    lax.fori_loop(0, half // CHUNK, first, 0)
    mix_pre = mm(zed[...], mix_in[...], NT)
    pre[...] = mix_pre
    act = (mix_pre * phi_parts(mix_pre)[0]).astype(BF16)
    weights[...] = mm(act, mix_out[...]) + mix_bias[...]

    def second(step, _):
        rows = pl.ds(pl.multiple_of(step * CHUNK, CHUNK), CHUNK)
        parts = [hist[source, rows, :].astype(F32) for source in range(entries)]
        mine = weights[rows, :]
        for stream in range(4):
            normed = norm_parts(mix_rows(parts, mine, stream))[0]
            at = 2 if stream == 3 else 0
            value = (normed * vecs[at : at + 1, :] + vecs[at + 1 : at + 2, :]).astype(BF16)
            for source, start, size in lane_blocks(width, nb, na):
                if stream == 3:
                    resid[rows, start : start + size] = value[:, source]
                else:
                    qkv[stream, rows, start : start + size] = value[:, source]
        return 0

    lax.fori_loop(0, half // CHUNK, second, 0)


def whole_spec(shape):
    return pl.BlockSpec(shape, lambda *_: (0,) * len(shape))


def local_forward(core, history, cotangent, vecs, mix_in, mix_out, mix_bias, nb, na, half):
    entries, _, width = history.shape
    hidden = mix_in.shape[0]
    outs = [
        ((3, half, width), BF16),
        ((half, width), BF16),
        ((half, width), BF16),
        ((half, LANES), F32),
        ((half, hidden), F32),
    ]
    return pl.pallas_call(
        functools.partial(local_forward_body, nb, na),
        out_shape=[jax.ShapeDtypeStruct(shape, kind) for shape, kind in outs],
        grid_spec=pltpu.PrefetchScalarGridSpec(
            num_scalar_prefetch=1,
            grid=(1,),
            in_specs=[
                pl.BlockSpec((entries, half, width), lambda i, core: (0, core[0], 0)),
                pl.BlockSpec((half, width), lambda i, core: (core[0], 0)),
                whole_spec(vecs.shape),
                whole_spec(mix_in.shape),
                whole_spec(mix_out.shape),
                whole_spec(mix_bias.shape),
            ],
            out_specs=[whole_spec(shape) for shape, _ in outs],
            scratch_shapes=[pltpu.VMEM((half, width), BF16)],
        ),
        cost_estimate=pl.CostEstimate(flops=60_000_000, bytes_accessed=4_000_000, transcendentals=0),
        name="local_forward",
    )(core, history, cotangent, vecs, mix_in, mix_out, mix_bias)


def local_backward_body(
    nb,
    na,
    core,
    hist,
    cot,
    vecs,
    mix_in,
    mix_out,
    weights,
    pre,
    own,
    got,
    moved_first,
    moved_last,
    own_resid,
    got_resid,
    moved_resid,
    bias_rows,
    grad_hist,
    block,
    small,
    zed,
    low,
    grad_zed,
    sums,
    misc,
):
    entries, half, width = hist.shape
    sums[...] = jnp.zeros_like(sums)
    misc[...] = jnp.zeros_like(misc)

    def first(step, _):
        rows = pl.ds(pl.multiple_of(step * CHUNK, CHUNK), CHUNK)
        parts = [hist[source, rows, :].astype(F32) for source in range(entries)]
        mine = weights[rows, :]
        last = parts[entries - 1]
        inverse = lax.rsqrt(jnp.mean(last * last, -1, keepdims=True) + EPS)
        zed[rows, :] = (last * inverse * vecs[4:5, :]).astype(BF16)
        cot_rows = cot[rows, :].astype(F32)
        sums[5:6, :] += jnp.sum(cot_rows, 0, keepdims=True)
        grads = []
        for stream in range(4):
            values = mix_rows(parts, mine, stream)
            normed, scale = norm_parts(values)
            if stream == 3:
                total = own_resid[0, rows, :] + got_resid[0, rows, :].astype(F32)
                total = total + moved_resid[rows, :].astype(F32)
                branch = own[0, 0, rows, :] + got[0, 0, rows, :].astype(F32)
                branch = from_gathered(branch + moved_first[0, rows, :].astype(F32), nb, na)
                block[rows, :] = (values + branch + vecs[5:6, :]).astype(BF16)
            else:
                total = own[0, stream + 1, rows, :] + got[0, stream + 1, rows, :].astype(F32)
                moved = moved_last[stream - 1, rows, :] if stream else moved_first[1, rows, :]
                total = total + moved.astype(F32)
            incoming = from_gathered(total, nb, na)
            at = 2 if stream == 3 else 0
            sums[at : at + 1, :] += jnp.sum(incoming * normed, 0, keepdims=True)
            sums[at + 1 : at + 2, :] += jnp.sum(incoming, 0, keepdims=True)
            grad = norm_back(incoming, normed, scale, vecs[at : at + 1, :])
            grads.append(grad + cot_rows if stream == 3 else grad)
        lane = lax.broadcasted_iota(jnp.int32, (CHUNK, LANES), 1)
        cells = jnp.zeros((CHUNK, LANES), F32)
        for stream in range(4):
            for source in range(entries):
                cell = jnp.sum(grads[stream] * parts[source], -1, keepdims=True)
                cells = jnp.where(lane == stream * entries + source, cell, cells)
        low[rows, :] = cells.astype(BF16)
        for source in range(entries):
            total = mine[:, source : source + 1] * grads[0]
            for stream in range(1, 4):
                at = stream * entries + source
                total = total + mine[:, at : at + 1] * grads[stream]
            grad_hist[source, rows, :] = total
        return 0

    lax.fori_loop(0, half // CHUNK, first, 0)
    grad_low = low[...]
    mix_pre = pre[...]
    cdf, pdf = phi_parts(mix_pre)
    act = (mix_pre * cdf).astype(BF16)
    rows_used = -(-68 // 8) * 8
    misc[: mix_in.shape[0], :] = mm(act, grad_low, TN)
    misc[rows_used : rows_used + 1, :] = jnp.sum(grad_low.astype(F32), 0, keepdims=True)
    mixed = weights[...]
    misc[rows_used + 1 : rows_used + 2, :] = jnp.sum(mixed, 0, keepdims=True)
    misc[rows_used + 2 : rows_used + 3, :] = jnp.sum(mixed * mixed, 0, keepdims=True)
    grad_act = mm(grad_low, mix_out[...], NT)
    grad_pre = (grad_act * (cdf + mix_pre * pdf)).astype(BF16)
    grad_in = mm(grad_pre, zed[...], TN)
    grad_zed[...] = mm(grad_pre, mix_in[...])

    def second(step, _):
        rows = pl.ds(pl.multiple_of(step * CHUNK, CHUNK), CHUNK)
        last = hist[entries - 1, rows, :].astype(F32)
        inverse = lax.rsqrt(jnp.mean(last * last, -1, keepdims=True) + EPS)
        normed = last * inverse
        incoming = grad_zed[rows, :]
        sums[4:5, :] += jnp.sum(incoming * normed, 0, keepdims=True)
        scaled = incoming * vecs[4:5, :]
        grad_last = inverse * (scaled - normed * jnp.mean(scaled * normed, -1, keepdims=True))
        grad_hist[entries - 1, rows, :] += grad_last
        return 0

    lax.fori_loop(0, half // CHUNK, second, 0)
    tiles = width // LANES
    per = misc.shape[0] // tiles
    count = small.shape[2]
    for tile in range(tiles):
        lanes = slice(tile * LANES, (tile + 1) * LANES)
        rows = jnp.concatenate(
            [
                grad_in[:rows_used, lanes],
                sums[:, lanes],
                misc[tile * per : (tile + 1) * per, :],
                bias_rows[tile],
            ],
            0,
        )
        for part in range(2):
            small[lax.bitwise_xor(core[0], part), tile] = rows[part * count : (part + 1) * count]


def local_backward(
    core, history, cotangent, vecs, mix_in, mix_out, weights, pre, own, got, moved_first, moved_last, own_resid,
    got_resid, moved_resid, bias_rows, nb, na, half,
):
    entries, _, width = history.shape
    tiles = width // LANES
    misc_rows = 8 * tiles
    outs = [
        ((entries, half, width), F32),
        ((half, width), BF16),
        ((2, tiles, (72 + 8 + 8 + bias_rows.shape[1]) // 2, LANES), F32),
    ]
    slot = pl.BlockSpec((1, 4, half, width), lambda i, core: (0, 0, 0, 0))
    slot_resid = pl.BlockSpec((1, half, width), lambda i, core: (0, 0, 0))
    return pl.pallas_call(
        functools.partial(local_backward_body, nb, na),
        out_shape=[jax.ShapeDtypeStruct(shape, kind) for shape, kind in outs],
        grid_spec=pltpu.PrefetchScalarGridSpec(
            num_scalar_prefetch=1,
            grid=(1,),
            in_specs=[
                pl.BlockSpec((entries, half, width), lambda i, core: (0, core[0], 0)),
                pl.BlockSpec((half, width), lambda i, core: (core[0], 0)),
                whole_spec(vecs.shape),
                whole_spec(mix_in.shape),
                whole_spec(mix_out.shape),
                whole_spec(weights.shape),
                whole_spec(pre.shape),
                slot,
                slot,
                whole_spec(moved_first.shape),
                whole_spec(moved_last.shape),
                slot_resid,
                slot_resid,
                whole_spec(moved_resid.shape),
                whole_spec(bias_rows.shape),
            ],
            out_specs=[whole_spec(shape) for shape, _ in outs],
            scratch_shapes=[
                pltpu.VMEM((half, width), BF16),
                pltpu.VMEM((half, LANES), BF16),
                pltpu.VMEM((half, width), F32),
                pltpu.VMEM((8, width), F32),
                pltpu.VMEM((misc_rows, LANES), F32),
            ],
        ),
        cost_estimate=pl.CostEstimate(flops=150_000_000, bytes_accessed=12_000_000, transcendentals=0),
        name="local_backward",
    )(
        core, history, cotangent, vecs, mix_in, mix_out, weights, pre, own, got, moved_first, moved_last, own_resid,
        got_resid, moved_resid, bias_rows,
    )


SENT_FIRST = {(1, 0): (0, 0), (3, 0): (0, 1), (2, 1): (1, 0), (3, 1): (1, 1)}
KEPT = {(0, 0): 2, (2, 0): 3, (0, 1): 4, (1, 1): 5}


def piece_of(refs, index):
    if len(refs) == 1:
        return refs[0]
    piece = divmod(index, 2)
    if piece in KEPT:
        return refs[KEPT[piece]]
    which, place = SENT_FIRST[piece]
    return refs[which].at[place]


def piece_outs(shape, square):
    return [(2, *shape)] * 2 + [shape] * 4 if square else [shape]


def block_starts(info, nb, na, width, relative, square):
    size = width // (nb * na)
    if size % LANES:
        return [i * LANES for i in range(width // LANES)], LANES
    starts = []
    for slot in range(na):
        row = lax.bitwise_xor(info[1], slot) if relative and square else slot
        for step in range(nb):
            line = info[2] - step
            line = jnp.where(line < 0, line + nb, line)
            starts.append(pl.multiple_of((row * nb + line) * size, size))
    return starts, size


def feed_forward_body(nb, na, square, info, *refs):
    x_slots, g_slots, refs = refs[: 2 * nb], refs[2 * nb : 4 * nb], refs[4 * nb :]
    count = 2 * na if square else 1
    ups, downs, bias, refs = refs[:count], refs[count : 2 * count], refs[2 * count], refs[2 * count + 1 :]
    count = 6 if square else 1
    grads_up, grads_down, refs = refs[:count], refs[count : 2 * count], refs[2 * count :]
    grad_bias, part_own, part_other, branch_own, branch_other = refs[:5]
    x_all, g_all, x_turned, part_sum, branch_sum = refs[5:]
    step = pl.program_id(0)
    half, width = x_slots[0].shape
    rows = nb * half
    starts, size = block_starts(info, nb, na, width, True, square)

    @pl.when(step == 0)
    def _():
        for i, start in enumerate(starts):
            at, lanes = slice(i * size, (i + 1) * size), pl.ds(start, size)
            for slot in range(2 * nb):
                mine = slice(slot * half, (slot + 1) * half)
                x_all[mine, at] = x_slots[slot][:, lanes]
                g_all[mine, at] = g_slots[slot][:, lanes]
            x_turned[at, :] = x_all[:, at].T

    up = jnp.concatenate([piece[...] for piece in ups], 0)
    up_pre = mm(x_all[...], up) + bias[...]
    cdf, pdf = phi_parts(up_pre)
    gelu_out = (up_pre * cdf).astype(BF16)
    wide = jnp.concatenate([piece[i] for piece in downs for i in range(piece.shape[0])], -1)
    grad_gelu = mm(g_all[...], wide, NT)
    grad_up = (grad_gelu * (cdf + up_pre * pdf)).astype(BF16)
    grad_bias[...] = jnp.sum(grad_up.astype(F32), 0, keepdims=True)
    grad = mm(x_turned[...], grad_up).astype(BF16)
    each = ups[0].shape[0]
    for index in range(len(ups)):
        piece_of(grads_up, index)[...] = grad[index * each : (index + 1) * each]
    grad = mm(gelu_out.T, g_all[...]).astype(BF16)
    each, _, lanes = downs[0].shape
    for index in range(len(downs)):
        piece = piece_of(grads_down, index)
        for i in range(each):
            at = (index * each + i) * lanes
            piece[i] = grad[:, at : at + lanes]
    part = mm(grad_up, up, NT)
    branch = mm(gelu_out, wide)

    @pl.when(step == 0)
    def _():
        part_sum[...] = part
        branch_sum[...] = branch

    @pl.when(step > 0)
    def _():
        part_sum[...] += part
        branch_sum[...] += branch

    @pl.when(step == pl.num_programs(0) - 1)
    def _():
        for i, start in enumerate(starts):
            at, lanes = slice(i * size, (i + 1) * size), pl.ds(start, size)
            part_own[:, lanes] = part_sum[:rows, at]
            part_other[:, lanes] = part_sum[rows:, at].astype(BF16)
            branch_own[:, lanes] = branch_sum[:rows, at]
            branch_other[:, lanes] = branch_sum[rows:, at]


def feed_forward(info, x_slots, g_slots, ups, downs, bias, nb, na, square):
    half, width = x_slots[0].shape
    rows = nb * half
    hidden = bias.shape[1]
    tile = 256

    def tiled(shape):
        dim = max(i for i, size in enumerate(shape) if size == hidden)
        block = tuple(tile if i == dim else size for i, size in enumerate(shape))
        return pl.BlockSpec(block, lambda j, info: tuple(j if i == dim else 0 for i in range(len(shape))))

    fixed = pl.BlockSpec((rows, width), lambda j, info: (0, 0), pipeline_mode=pl.Buffered(1))
    outs = [(shape, BF16, tiled(shape)) for shape in piece_outs(ups[0].shape, square)]
    outs += [(shape, BF16, tiled(shape)) for shape in piece_outs(downs[0].shape, square)]
    outs += [
        ((1, hidden), F32, tiled((1, hidden))),
        ((rows, width), F32, fixed),
        ((rows, width), BF16, fixed),
        ((rows, width), F32, fixed),
        ((rows, width), F32, fixed),
    ]
    results = pl.pallas_call(
        functools.partial(feed_forward_body, nb, na, square),
        out_shape=[jax.ShapeDtypeStruct(shape, kind) for shape, kind, _ in outs],
        grid_spec=pltpu.PrefetchScalarGridSpec(
            num_scalar_prefetch=1,
            grid=(hidden // tile,),
            in_specs=[pl.BlockSpec((half, width), lambda j, info: (0, 0), pipeline_mode=pl.Buffered(1))] * (4 * nb)
            + [tiled(value.shape) for value in (*ups, *downs, bias)],
            out_specs=[spec for _, _, spec in outs],
            scratch_shapes=[
                pltpu.VMEM((2 * rows, width), BF16),
                pltpu.VMEM((2 * rows, width), BF16),
                pltpu.VMEM((width, 2 * rows), BF16),
                pltpu.VMEM((2 * rows, width), F32),
                pltpu.VMEM((2 * rows, width), F32),
            ],
        ),
        compiler_params=pltpu.CompilerParams(vmem_limit_bytes=60 * 1024 * 1024),
        cost_estimate=pl.CostEstimate(
            flops=24 * rows * width * hidden, bytes_accessed=32_000_000, transcendentals=4 * rows * hidden
        ),
        name="feed_forward",
    )(info, *x_slots, *g_slots, *ups, *downs, bias)
    count = 6 if square else 1
    return results[:count], results[count : 2 * count], *results[2 * count :]


def rotary_tables(length):
    half_rot = ROT // 2
    frequency = np.exp(np.arange(half_rot) * (-2.0 * math.log(10000.0) / ROT))
    angles = np.arange(length)[:, None] * frequency[None, :]
    tables = np.zeros((3, length, HEAD_DIM), np.float32)
    tables[0] = 1.0
    tables[0, :, :half_rot] = tables[0, :, half_rot:ROT] = np.cos(angles)
    tables[1, :, half_rot:ROT] = np.sin(angles)
    tables[2, :, :half_rot] = -np.sin(angles)
    return tables


def turn(values, cosine, rising, falling):
    half_rot = ROT // 2
    return (
        values * cosine
        + pltpu.roll(values, half_rot, 1) * rising
        + pltpu.roll(values, HEAD_DIM - half_rot, 1) * falling
    )


def attention_body(seqs, na, square, info, *refs):
    x_slots, g_slots, refs = refs[: 2 * seqs], refs[2 * seqs : 4 * seqs], refs[4 * seqs :]
    count = 2 * na if square else 1
    pieces, refs = refs[:count], refs[count:]
    bias, tables, branch_own, branch_other = refs[:4]
    count = 6 if square else 1
    grads, refs = refs[4 : 4 + count], refs[4 + count :]
    grad_bias, own = refs[:2]
    others, refs = refs[2 : 2 + seqs], refs[2 + seqs :]
    pre, table, mixed, grad_mixed, grad_pre, x_turned, out_w, weights, g_turned, x_all, g_all = refs
    core = info
    _, half, width = x_slots[0].shape
    starts, size = block_starts(info, seqs, na, width, True, square)
    part_rows = pieces[0].shape[0]
    per = part_rows // size
    for i, start in enumerate(starts):
        weights[pl.ds(start, size), :] = pieces[i // per][i % per * size : (i % per + 1) * size, :]

    def store_grad(row, lanes, value):
        at = slice(row % part_rows, row % part_rows + value.shape[0])
        piece_of(grads, row // part_rows)[at, lanes] = value.astype(BF16)

    length = 2 * half
    cols = bias.shape[1] // 3
    heads = cols // HEAD_DIM
    blocks = weights.shape[0] // LANES
    first = pl.multiple_of(core[0] * half, half)
    second = pl.multiple_of((1 - core[0]) * half, half)
    for kind in range(3):
        table[kind, :half] = tables[kind, pl.ds(first, half), :]
        table[kind, half:] = tables[kind, pl.ds(second, half), :]

    for slot in range(2 * seqs):
        at = slot % seqs * length + slot // seqs * half
        x_all[:, at : at + half, :] = x_slots[slot][...]
        g_all[at : at + half, :] = g_slots[slot][...]
    for kind in range(3):
        lanes = slice(kind * cols, (kind + 1) * cols)
        pre[kind] = mm(x_all[kind], weights[:, lanes]) + bias[:, lanes]

    for i in range(blocks):
        for part in range(cols // LANES):
            at = 3 * cols + part * LANES
            out_w[part * LANES : (part + 1) * LANES, i * LANES : (i + 1) * LANES] = weights[
                i * LANES : (i + 1) * LANES, at : at + LANES
            ]
    grad_mixed[0] = mm(g_all[...], out_w[...], NT)

    scale = HEAD_DIM ** (-0.5)
    row = lax.broadcasted_iota(jnp.int32, (length, length), 0)
    col = lax.broadcasted_iota(jnp.int32, (length, length), 1)
    row_at = jnp.where(row < half, row + core[0] * half, row - core[0] * half)
    col_at = jnp.where(col < half, col + core[0] * half, col - core[0] * half)
    causal = row_at >= col_at

    def one_seq(seq, _):
        at = pl.ds(pl.multiple_of(seq * length, length), length)
        cosine, rising, falling = table[0], table[1], table[2]
        for head in range(heads):
            lanes = slice(head * HEAD_DIM, (head + 1) * HEAD_DIM)
            query = turn(pre[0, at, lanes], cosine, rising, falling).astype(BF16)
            key = turn(pre[1, at, lanes], cosine, rising, falling).astype(BF16)
            value = pre[2, at, lanes].astype(BF16)
            scores = jnp.where(causal, mm(query, key, NT) * scale, -1e30)
            expon = jnp.exp(scores - jnp.max(scores, -1, keepdims=True))
            probs = expon / jnp.sum(expon, -1, keepdims=True)
            low = probs.astype(BF16)
            mixed[at, lanes] = mm(low, value).astype(BF16)
            grad = grad_mixed[0, at, lanes].astype(BF16)
            grad_value = mm(low, grad, TN)
            grad_probs = mm(grad, value, NT)
            delta = jnp.sum(probs * grad_probs, -1, keepdims=True)
            grad_scores = (probs * (grad_probs - delta)).astype(BF16)
            grad_query = mm(grad_scores, key) * scale
            grad_key = mm(grad_scores, query, TN) * scale
            grad_pre[0, at, lanes] = turn(grad_query, cosine, -rising, -falling).astype(BF16)
            grad_pre[1, at, lanes] = turn(grad_key, cosine, -rising, -falling).astype(BF16)
            grad_pre[2, at, lanes] = grad_value.astype(BF16)
        return 0

    lax.fori_loop(0, seqs, one_seq, 0)

    for i in range(blocks):
        g_turned[:, i * LANES : (i + 1) * LANES] = g_all[:, pl.ds(starts[i], LANES)]
    mixed_all = mixed[...]
    for seq in range(seqs):
        at, mid = seq * length, seq * length + half
        rows_own = slice(seq * half, (seq + 1) * half)
        own[seq, 0] = branch_own[rows_own] + mm(mixed_all[at:mid], out_w[...])
        others[seq][0] = (branch_other[rows_own] + mm(mixed_all[mid : mid + half], out_w[...])).astype(BF16)
    grad_out = mm(mixed_all.T, g_turned[...])
    for i in range(blocks):
        for part in range(cols // LANES):
            at = 3 * cols + part * LANES
            store_grad(
                i * LANES,
                slice(at, at + LANES),
                grad_out[part * LANES : (part + 1) * LANES, i * LANES : (i + 1) * LANES],
            )
    for kind in range(3):
        grad = grad_pre[kind]
        grad_bias[:, kind * cols : (kind + 1) * cols] = jnp.sum(grad.astype(F32), 0, keepdims=True)
        for i in range(blocks):
            x_turned[i * LANES : (i + 1) * LANES, :] = x_all[kind, :, pl.ds(starts[i], LANES)].T
        for start in range(0, width, part_rows):
            store_grad(
                start,
                slice(kind * cols, (kind + 1) * cols),
                mm(x_turned[start : start + part_rows, :], grad),
            )
        part = mm(grad, weights[:, kind * cols : (kind + 1) * cols], NT)
        for seq in range(seqs):
            at, mid = seq * length, seq * length + half
            own[seq, kind + 1] = part[at:mid]
            others[seq][kind + 1] = part[mid : mid + half].astype(BF16)


def attention(info, x_slots, g_slots, pieces, bias, tables, branch_own, branch_other, seqs, na, square):
    _, half, width = x_slots[0].shape
    rows = seqs * half
    cols = bias.shape[1] // 3
    piece = pieces[0].shape
    outs = [(shape, BF16) for shape in piece_outs(piece, square)]
    outs += [(bias.shape, F32), ((seqs, 4, half, width), F32)]
    outs += [((4, half, width), BF16)] * seqs
    operands = (*x_slots, *g_slots, *pieces, bias, tables, branch_own, branch_other)
    one = lambda shape: pl.BlockSpec(shape, lambda *_: (0,) * len(shape), pipeline_mode=pl.Buffered(1))
    return pl.pallas_call(
        functools.partial(attention_body, seqs, na, square),
        out_shape=[jax.ShapeDtypeStruct(shape, kind) for shape, kind in outs],
        grid_spec=pltpu.PrefetchScalarGridSpec(
            num_scalar_prefetch=1,
            grid=(1,),
            in_specs=[one(value.shape) for value in operands],
            out_specs=[one(shape) for shape, _ in outs],
            scratch_shapes=[
                pltpu.VMEM((3, 2 * rows, cols), F32),
                pltpu.VMEM((3, 2 * half, HEAD_DIM), F32),
                pltpu.VMEM((2 * rows, cols), BF16),
                pltpu.VMEM((1, 2 * rows, cols), F32),
                pltpu.VMEM((3, 2 * rows, cols), BF16),
                pltpu.VMEM((width, 2 * rows), BF16),
                pltpu.VMEM((cols, width), BF16),
                pltpu.VMEM((width, piece[1]), BF16),
                pltpu.VMEM((2 * rows, width), BF16),
                pltpu.VMEM((3, 2 * rows, width), BF16),
                pltpu.VMEM((2 * rows, width), BF16),
            ],
        ),
        compiler_params=pltpu.CompilerParams(vmem_limit_bytes=62 * 1024 * 1024),
        cost_estimate=pl.CostEstimate(
            flops=48 * rows * width * cols, bytes_accessed=32_000_000, transcendentals=rows * cols
        ),
        name="attention",
    )(info, *operands)


def ring(values):
    return shift_b(values, 1)


def swap_core(values):
    return lax.ppermute(values, "mp", SWAP)


def shift_b(values, step):
    size = lax.axis_size("b")
    return lax.ppermute(values, "b", [(i, (i + step) % size) for i in range(size)])


def exchange_b(block_of):
    nb, line = lax.axis_size("b"), lax.axis_index("b")
    slots = [block_of(lax.rem(line + step, nb)) for step in range(nb)]
    return [shift_b(block, step) if step else block for step, block in enumerate(slots)]


def by_line(slots):
    nb, line = lax.axis_size("b"), lax.axis_index("b")
    blocks = jnp.stack(slots)
    return [lax.dynamic_index_in_dim(blocks, lax.rem(line - i + nb, nb), 0, keepdims=False) for i in range(nb)]


def gather_a(blocks):
    return lax.all_gather(blocks, "a", axis=0, tiled=True)


def across(values, bits):
    return lax.ppermute(values, "a", [(i, i ^ bits) for i in range(lax.axis_size("a"))])


def gather_square(slots):
    middle = len(slots) // 2
    first, second = jnp.concatenate(slots[:middle]), jnp.concatenate(slots[middle:])
    first_x, second_y = across(first, 1), across(second, 2)
    first_y, second_x = across(first, 2), across(second, 1)
    first_xy, second_xy = across(first_x, 2), across(second_y, 1)
    return [first, second, first_x, second_x, first_y, second_y, first_xy, second_xy]


def scatter_square(grads, nb):
    sent_x, sent_y, first, first_y, second, second_x = grads
    got_x, got_y = across(sent_x, 1), across(sent_y, 2)
    add = lambda left, right: left.astype(F32) + right.astype(F32)
    first_y = across(add(first_y, got_x[1]).astype(BF16), 2)
    second_x = across(add(second_x, got_y[1]).astype(BF16), 1)
    blocks = []
    per = nb // 2
    each = first.shape[0] // per
    for kept, got, last in ((first, got_x[0], first_y), (second, got_y[0], second_x)):
        for i in range(per):
            at = slice(i * each, (i + 1) * each)
            blocks.append(add(kept[at], got[at]) + last[at].astype(F32))
    return blocks


def scatter_a(grad):
    return lax.psum_scatter(grad, "a", scatter_dimension=0, tiled=True)


def grads_home(mine):
    nb = lax.axis_size("b")
    return [shift_b(mine[step].astype(BF16), -step) if step else mine[0] for step in range(nb)]


def place(slots, axis):
    nb = len(slots)
    line = lax.axis_index("b")
    size = slots[0].shape[axis]
    shape = list(slots[0].shape)
    shape[axis] *= nb
    out = jnp.zeros(shape, F32)
    for step, slot in enumerate(slots):
        at = lax.rem(line + step, nb) * size
        out = lax.dynamic_update_slice_in_dim(out, slot.astype(F32), at, axis)
    return out


def place_vector(values, full_len, index):
    return lax.dynamic_update_slice_in_dim(
        jnp.zeros((full_len,), F32), values, index * values.shape[0], 0
    )


def sum_small(small):
    tiles = small.shape[1]
    dp = ("b", "a")
    mine = small[0] + swap_core(small[1])
    if lax.axis_size(dp) == tiles:
        blocks = lax.all_to_all(mine, dp, 0, 0, tiled=True)
        mine = lax.all_to_all(jnp.broadcast_to(jnp.sum(blocks, 0), mine.shape), dp, 0, 0, tiled=True)
    else:
        mine = lax.psum(mine, dp)
    other = swap_core(mine)
    first = lax.axis_index("mp") == 0
    return jnp.concatenate([jnp.where(first, mine, other), jnp.where(first, other, mine)], 1)


def shards(
    history, cotangent, weight_query, weight_key, weight_value, weight_out, weight_up, weight_down,
    bias_query, bias_key, bias_value, out_bias, bias_up, attn_gain, attn_shift, mlp_gain, mlp_shift,
    mix_gain, mix_in, mix_out, mix_bias,
):
    _, length, width = history.shape
    nb, na, n_mp = lax.axis_size("b"), lax.axis_size("a"), lax.axis_size("mp")
    line, core = lax.axis_index("b"), lax.axis_index("mp")
    half = length // n_mp
    own_rows = width // (nb * na)
    mix_hid = mix_in.shape[1]
    core_ref = jnp.stack([core, lax.axis_index("a"), line]).astype(jnp.int32)
    square = na == 4

    hidden = weight_up.shape[1] // nb
    up_slots = exchange_b(lambda i: lax.dynamic_slice_in_dim(weight_up, i * hidden, hidden, 1))
    whole_lanes = own_rows % LANES == 0
    line_order = (lambda slots: slots) if whole_lanes else by_line
    if square:
        full_up = gather_square(up_slots)
    else:
        full_up = [gather_a(jnp.stack(line_order(up_slots))).reshape(width, -1)]

    vecs = jnp.stack([attn_gain, attn_shift, mlp_gain, mlp_shift, mix_gain, out_bias]).astype(F32)
    mix_in_t = jnp.pad(mix_in.T, ((0, LANES - mix_hid), (0, 0)))
    mix_out_p = jnp.pad(mix_out, ((0, LANES - mix_hid), (0, LANES - mix_out.shape[1])))
    mix_bias_p = jnp.pad(mix_bias.astype(F32), (0, LANES - mix_bias.shape[0])).reshape(1, LANES)
    in_qkv, in_resid, cot, mix_weights, mix_pre = local_forward(
        core_ref, history, cotangent, vecs, mix_in_t, mix_out_p, mix_bias_p, nb, na, half
    )

    down = weight_down
    down_slots = exchange_b(lambda i: lax.dynamic_slice_in_dim(down, i * hidden, hidden, 0))
    if square:
        full_down = gather_square([slot[None] for slot in down_slots])
    else:
        full_down = [gather_a(jnp.stack(line_order(down_slots)))]

    def gather_tokens(values):
        slots = [values]
        for _ in range(1, nb):
            slots.append(ring(slots[-1]))
        return [*slots, *(swap_core(slot) for slot in slots)]

    g_slots = gather_tokens(cot)
    x_slots = gather_tokens(in_resid)
    qkv_slots = gather_tokens(in_qkv)

    bias_up_mine = lax.dynamic_slice_in_dim(bias_up, line * hidden, hidden, 0).astype(F32)
    grad_up, grad_down, grad_bias_up, part_own, part_other, branch_own, branch_other = feed_forward(
        core_ref, x_slots, g_slots, full_up, full_down, bias_up_mine.reshape(1, -1), nb, na, square
    )

    def scatter_tokens(mine, theirs):
        moving = mine[1] + theirs[1].astype(F32)
        for step in range(2, nb):
            moving = ring(moving.astype(BF16)).astype(F32) + (mine[step] + theirs[step].astype(F32))
        return ring(moving.astype(BF16))

    def send_home(mine, theirs):
        total = 0.0
        for step in range(1, nb):
            pair = (mine[step] + theirs[step].astype(F32)).astype(BF16)
            total = total + shift_b(pair, -step).astype(F32)
        return total

    part_own = part_own.reshape(nb, half, width)
    got_resid = swap_core(part_other.reshape(nb, half, width))
    moved_resid = send_home(part_own, got_resid)
    head_cols = weight_query.shape[1] // nb
    groups = head_cols // HEAD_DIM
    pieces = [w.reshape(own_rows, nb, head_cols).transpose(1, 0, 2) for w in (weight_query, weight_key, weight_value)]
    out_blocks = weight_out.reshape(nb, groups, HEAD_DIM, own_rows)
    packed = own_rows == LANES
    if not packed:
        out_blocks = weight_out.reshape(nb, head_cols, own_rows).transpose(0, 2, 1)
        pieces.append(out_blocks)
    else:
        pieces.extend(out_blocks[:, group] for group in range(groups))
    attn_blocks = jnp.concatenate(pieces, -1)
    attn_slots = exchange_b(lambda i: lax.dynamic_index_in_dim(attn_blocks, i, 0, keepdims=False))
    if square:
        full_attn = gather_square(attn_slots)
    else:
        full_attn = [gather_a(jnp.stack(line_order(attn_slots))).reshape(width, -1)]
    biases = [
        lax.dynamic_slice_in_dim(bias, line * head_cols, head_cols, 0).astype(F32)
        for bias in (bias_query, bias_key, bias_value)
    ]
    if not packed:
        full_attn = [repack_out(full_attn[0], head_cols, True)]
    results = attention(
        core_ref, qkv_slots, g_slots, full_attn, jnp.concatenate(biases).reshape(1, -1),
        jnp.asarray(rotary_tables(length)), branch_own, branch_other, nb, na, square,
    )
    other = results[-nb:]
    *grad_attn, grad_bias_attn, own = results[:-nb]

    got = {slot: swap_core(other[slot]) for slot in (*range(1, nb), 0)}
    moved_first = scatter_tokens(own[:, :2], {slot: got[slot][:2] for slot in got})
    moved_last = scatter_tokens(own[:, 2:], {slot: got[slot][2:] for slot in got})

    block = core * nb + line
    tiles = width // LANES
    rows_of = lambda value, full: place_vector(value, full, block).reshape(-1, tiles, LANES).transpose(1, 0, 2)
    bias_rows = [rows_of(grad_bias_up.reshape(-1), bias_up.shape[0] * n_mp)]
    for kind in range(3):
        bias_rows.append(rows_of(grad_bias_attn[0, kind * head_cols : (kind + 1) * head_cols], width))
    bias_rows = jnp.concatenate(bias_rows, 1)
    bias_count = bias_rows.shape[1]
    bias_rows = jnp.pad(bias_rows, ((0, 0), (0, -bias_count % 16 if bias_count % 16 > 8 else -bias_count % 8), (0, 0)))

    grad_history, block_half, small = local_backward(
        core_ref, history, cotangent, vecs, mix_in_t, mix_out_p, mix_weights, mix_pre, own, got[0][None], moved_first, moved_last,
        part_own, got_resid, moved_resid, bias_rows, nb, na, half,
    )
    block_other = swap_core(block_half)
    first = core == 0
    block_out = jnp.concatenate(
        [jnp.where(first, block_half, block_other), jnp.where(first, block_other, block_half)], 0
    )
    small = sum_small(small)

    if square:
        up_sum = scatter_square(grad_up, nb)
        down_sum = [block.reshape(-1, own_rows) for block in scatter_square(grad_down, nb)]
        attn_sum = scatter_square(grad_attn, nb)
    else:
        up_sum = scatter_a(grad_up[0].reshape(na * nb, own_rows, -1))
        down_sum = scatter_a(grad_down[0])
        grad_attn = grad_attn[0]
        if not packed:
            grad_attn = repack_out(grad_attn, head_cols, False)
        attn_sum = scatter_a(grad_attn.reshape(na * nb, own_rows, -1))
        up_sum, down_sum, attn_sum = (line_order(value) for value in (up_sum, down_sum, attn_sum))
    up_shard = place(grads_home(up_sum), 1)
    down_shard = place(grads_home(down_sum), 0)
    attn_slots = grads_home(attn_sum)
    shards_qkv = [
        place([slot[:, kind * head_cols : (kind + 1) * head_cols] for slot in attn_slots], 1)
        for kind in range(3)
    ]
    if packed:
        out_slots = [
            jnp.concatenate(
                [slot[:, 3 * head_cols + g * LANES : 3 * head_cols + (g + 1) * LANES] for g in range(groups)], 0
            )
            for slot in attn_slots
        ]
    else:
        out_slots = [slot[:, 3 * head_cols :].T for slot in attn_slots]
    out_shard = place(out_slots, 0)

    line_of = lambda row: small[:, row, :].reshape(-1)
    misc = small[:, 80:88, :].reshape(-1, LANES)
    tokens = length * nb * na
    n_mix = mix_bias.shape[0]
    mean_weights = misc[73, :n_mix] / tokens
    var_weights = misc[74, :n_mix] / tokens - mean_weights * mean_weights
    up_rows = bias_up.shape[0] * n_mp // width
    biases = small[:, 88 : 88 + bias_count, :].transpose(1, 0, 2).reshape(bias_count, width)
    return (
        block_out,
        grad_history,
        *shards_qkv,
        out_shard,
        up_shard,
        down_shard,
        biases[up_rows],
        biases[up_rows + 1],
        biases[up_rows + 2],
        line_of(77),
        biases[:up_rows].reshape(-1),
        line_of(72),
        line_of(73),
        line_of(74),
        line_of(75),
        line_of(76),
        small[:, :mix_hid, :].transpose(1, 0, 2).reshape(mix_hid, width).T,
        misc[:mix_hid, :n_mix],
        misc[72, :n_mix],
        jnp.stack([mean_weights, var_weights]),
    )


def repack_out(weights, cols, forward):
    width = weights.shape[0]
    lead, part = weights[:, : 3 * cols], weights[:, 3 * cols :]
    part = part.reshape(width // LANES, LANES, cols // LANES, LANES).transpose(0, 3, 2, 1)
    del forward
    return jnp.concatenate([lead, part.reshape(width, cols)], 1)


def solution(mesh):
    n_dp, n_mp = mesh.shape["dp"], mesh.shape["mp"]
    fine = Mesh(mesh.devices.reshape(NB, n_dp // NB, n_mp), ("b", "a", "mp"))
    dp = ("b", "a")
    whole = P()
    in_specs = (
        P(None, dp, None),
        P(dp, None),
        P(dp, "mp"),
        P(dp, "mp"),
        P(dp, "mp"),
        P("mp", dp),
        P(dp, "mp"),
        P("mp", dp),
        P("mp"),
        P("mp"),
        P("mp"),
        whole,
        P("mp"),
    ) + (whole,) * 8
    out_specs = (
        P(dp, None),
        P(None, dp + ("mp",), None),
        P(dp, "mp"),
        P(dp, "mp"),
        P(dp, "mp"),
        P("mp", dp),
        P(dp, "mp"),
        P("mp", dp),
    ) + (whole,) * 14
    return jax.shard_map(shards, mesh=fine, in_specs=in_specs, out_specs=out_specs, check_vma=False)
```

```python
import functools
import math

import jax
import jax.numpy as jnp
import numpy as np
from jax import lax
from jax.experimental import pallas as pl
from jax.experimental.pallas import tpu as pltpu
from jax.sharding import Mesh, PartitionSpec as P


HEAD_DIM = 128
ROT = 32
EPS = 1e-05
NB = 4
LANES = 128
CHUNK = 16
SWAP = ((0, 1), (1, 0))
F32 = jnp.float32
BF16 = jnp.bfloat16
NN, NT, TN = ((1,), (0,)), ((1,), (1,)), ((0,), (0,))


def mm(left, right, dims=NN):
    return lax.dot_general(left, right, (dims, ((), ())), preferred_element_type=F32)


def norm_parts(values):
    center = values - jnp.mean(values, -1, keepdims=True)
    inverse = lax.rsqrt(jnp.mean(center * center, -1, keepdims=True) + EPS)
    return center * inverse, inverse


def norm_back(grad_out, normed, inverse, gain):
    scaled = grad_out * gain
    return inverse * (
        scaled
        - jnp.mean(scaled, -1, keepdims=True)
        - normed * jnp.mean(scaled * normed, -1, keepdims=True)
    )


def phi_parts(values):
    cdf = 0.5 * (1.0 + lax.erf(values * (1.0 / math.sqrt(2.0))))
    pdf = jnp.exp(-0.5 * values * values) * (1.0 / math.sqrt(2.0 * math.pi))
    return cdf, pdf


def lane_blocks(width, nb, na):
    size = width // (nb * na)
    return [
        (slice((b * na + a) * size, (b * na + a + 1) * size), (a * nb + b) * size, size)
        for a in range(na)
        for b in range(nb)
    ]


def from_gathered(values, nb, na):
    blocks = sorted(lane_blocks(values.shape[-1], nb, na), key=lambda item: item[0].start)
    return jnp.concatenate([values[:, at : at + size] for _, at, size in blocks], -1)


def mix_rows(hist, weights, stream):
    entries = len(hist)
    total = weights[:, stream * entries : stream * entries + 1] * hist[0]
    for source in range(1, entries):
        at = stream * entries + source
        total = total + weights[:, at : at + 1] * hist[source]
    return total


def local_forward_body(
    nb, na, core, hist, cot, vecs, mix_in, mix_out, mix_bias, qkv, resid, cot_out, weights, pre, zed
):
    entries, half, width = hist.shape
    del core

    def first(step, _):
        rows = pl.ds(pl.multiple_of(step * CHUNK, CHUNK), CHUNK)
        last = hist[entries - 1, rows, :].astype(F32)
        inverse = lax.rsqrt(jnp.mean(last * last, -1, keepdims=True) + EPS)
        zed[rows, :] = (last * inverse * vecs[4:5, :]).astype(BF16)
        value = cot[rows, :]
        for source, at, size in lane_blocks(width, nb, na):
            cot_out[rows, at : at + size] = value[:, source]
        return 0

    lax.fori_loop(0, half // CHUNK, first, 0)
    mix_pre = mm(zed[...], mix_in[...], NT)
    pre[...] = mix_pre
    act = (mix_pre * phi_parts(mix_pre)[0]).astype(BF16)
    weights[...] = mm(act, mix_out[...]) + mix_bias[...]

    def second(step, _):
        rows = pl.ds(pl.multiple_of(step * CHUNK, CHUNK), CHUNK)
        parts = [hist[source, rows, :].astype(F32) for source in range(entries)]
        mine = weights[rows, :]
        for stream in range(4):
            normed = norm_parts(mix_rows(parts, mine, stream))[0]
            at = 2 if stream == 3 else 0
            value = (normed * vecs[at : at + 1, :] + vecs[at + 1 : at + 2, :]).astype(BF16)
            for source, start, size in lane_blocks(width, nb, na):
                if stream == 3:
                    resid[rows, start : start + size] = value[:, source]
                else:
                    qkv[stream, rows, start : start + size] = value[:, source]
        return 0

    lax.fori_loop(0, half // CHUNK, second, 0)


def whole_spec(shape):
    return pl.BlockSpec(shape, lambda *_: (0,) * len(shape))


def local_forward(core, history, cotangent, vecs, mix_in, mix_out, mix_bias, nb, na, half):
    entries, _, width = history.shape
    hidden = mix_in.shape[0]
    outs = [
        ((3, half, width), BF16),
        ((half, width), BF16),
        ((half, width), BF16),
        ((half, LANES), F32),
        ((half, hidden), F32),
    ]
    return pl.pallas_call(
        functools.partial(local_forward_body, nb, na),
        out_shape=[jax.ShapeDtypeStruct(shape, kind) for shape, kind in outs],
        grid_spec=pltpu.PrefetchScalarGridSpec(
            num_scalar_prefetch=1,
            grid=(1,),
            in_specs=[
                pl.BlockSpec((entries, half, width), lambda i, core: (0, core[0], 0)),
                pl.BlockSpec((half, width), lambda i, core: (core[0], 0)),
                whole_spec(vecs.shape),
                whole_spec(mix_in.shape),
                whole_spec(mix_out.shape),
                whole_spec(mix_bias.shape),
            ],
            out_specs=[whole_spec(shape) for shape, _ in outs],
            scratch_shapes=[pltpu.VMEM((half, width), BF16)],
        ),
        cost_estimate=pl.CostEstimate(flops=60_000_000, bytes_accessed=4_000_000, transcendentals=0),
        name="local_forward",
    )(core, history, cotangent, vecs, mix_in, mix_out, mix_bias)


def local_backward_body(
    nb,
    na,
    core,
    hist,
    cot,
    vecs,
    mix_in,
    mix_out,
    weights,
    pre,
    own,
    got,
    moved_first,
    moved_last,
    own_resid,
    got_resid,
    moved_resid,
    bias_rows,
    grad_hist,
    block,
    small,
    zed,
    low,
    grad_zed,
    sums,
    misc,
):
    entries, half, width = hist.shape
    sums[...] = jnp.zeros_like(sums)
    misc[...] = jnp.zeros_like(misc)

    def first(step, _):
        rows = pl.ds(pl.multiple_of(step * CHUNK, CHUNK), CHUNK)
        parts = [hist[source, rows, :].astype(F32) for source in range(entries)]
        mine = weights[rows, :]
        last = parts[entries - 1]
        inverse = lax.rsqrt(jnp.mean(last * last, -1, keepdims=True) + EPS)
        zed[rows, :] = (last * inverse * vecs[4:5, :]).astype(BF16)
        cot_rows = cot[rows, :].astype(F32)
        sums[5:6, :] += jnp.sum(cot_rows, 0, keepdims=True)
        grads = []
        for stream in range(4):
            values = mix_rows(parts, mine, stream)
            normed, scale = norm_parts(values)
            if stream == 3:
                total = own_resid[0, rows, :] + got_resid[0, rows, :].astype(F32)
                total = total + moved_resid[rows, :].astype(F32)
                branch = own[0, 0, rows, :] + got[0, 0, rows, :].astype(F32)
                branch = from_gathered(branch + moved_first[0, rows, :].astype(F32), nb, na)
                block[rows, :] = (values + branch + vecs[5:6, :]).astype(BF16)
            else:
                total = own[0, stream + 1, rows, :] + got[0, stream + 1, rows, :].astype(F32)
                moved = moved_last[stream - 1, rows, :] if stream else moved_first[1, rows, :]
                total = total + moved.astype(F32)
            incoming = from_gathered(total, nb, na)
            at = 2 if stream == 3 else 0
            sums[at : at + 1, :] += jnp.sum(incoming * normed, 0, keepdims=True)
            sums[at + 1 : at + 2, :] += jnp.sum(incoming, 0, keepdims=True)
            grad = norm_back(incoming, normed, scale, vecs[at : at + 1, :])
            grads.append(grad + cot_rows if stream == 3 else grad)
        lane = lax.broadcasted_iota(jnp.int32, (CHUNK, LANES), 1)
        cells = jnp.zeros((CHUNK, LANES), F32)
        for stream in range(4):
            for source in range(entries):
                cell = jnp.sum(grads[stream] * parts[source], -1, keepdims=True)
                cells = jnp.where(lane == stream * entries + source, cell, cells)
        low[rows, :] = cells.astype(BF16)
        for source in range(entries):
            total = mine[:, source : source + 1] * grads[0]
            for stream in range(1, 4):
                at = stream * entries + source
                total = total + mine[:, at : at + 1] * grads[stream]
            grad_hist[source, rows, :] = total
        return 0

    lax.fori_loop(0, half // CHUNK, first, 0)
    grad_low = low[...]
    mix_pre = pre[...]
    cdf, pdf = phi_parts(mix_pre)
    act = (mix_pre * cdf).astype(BF16)
    rows_used = -(-68 // 8) * 8
    misc[: mix_in.shape[0], :] = mm(act, grad_low, TN)
    misc[rows_used : rows_used + 1, :] = jnp.sum(grad_low.astype(F32), 0, keepdims=True)
    mixed = weights[...]
    misc[rows_used + 1 : rows_used + 2, :] = jnp.sum(mixed, 0, keepdims=True)
    misc[rows_used + 2 : rows_used + 3, :] = jnp.sum(mixed * mixed, 0, keepdims=True)
    grad_act = mm(grad_low, mix_out[...], NT)
    grad_pre = (grad_act * (cdf + mix_pre * pdf)).astype(BF16)
    grad_in = mm(grad_pre, zed[...], TN)
    grad_zed[...] = mm(grad_pre, mix_in[...])

    def second(step, _):
        rows = pl.ds(pl.multiple_of(step * CHUNK, CHUNK), CHUNK)
        last = hist[entries - 1, rows, :].astype(F32)
        inverse = lax.rsqrt(jnp.mean(last * last, -1, keepdims=True) + EPS)
        normed = last * inverse
        incoming = grad_zed[rows, :]
        sums[4:5, :] += jnp.sum(incoming * normed, 0, keepdims=True)
        scaled = incoming * vecs[4:5, :]
        grad_last = inverse * (scaled - normed * jnp.mean(scaled * normed, -1, keepdims=True))
        grad_hist[entries - 1, rows, :] += grad_last
        return 0

    lax.fori_loop(0, half // CHUNK, second, 0)
    tiles = width // LANES
    per = misc.shape[0] // tiles
    count = small.shape[2]
    for tile in range(tiles):
        lanes = slice(tile * LANES, (tile + 1) * LANES)
        rows = jnp.concatenate(
            [
                grad_in[:rows_used, lanes],
                sums[:, lanes],
                misc[tile * per : (tile + 1) * per, :],
                bias_rows[tile],
            ],
            0,
        )
        for part in range(2):
            small[lax.bitwise_xor(core[0], part), tile] = rows[part * count : (part + 1) * count]


def local_backward(
    core, history, cotangent, vecs, mix_in, mix_out, weights, pre, own, got, moved_first, moved_last, own_resid,
    got_resid, moved_resid, bias_rows, nb, na, half,
):
    entries, _, width = history.shape
    tiles = width // LANES
    misc_rows = 8 * tiles
    outs = [
        ((entries, half, width), F32),
        ((half, width), BF16),
        ((2, tiles, (72 + 8 + 8 + bias_rows.shape[1]) // 2, LANES), F32),
    ]
    slot = pl.BlockSpec((1, 4, half, width), lambda i, core: (0, 0, 0, 0))
    slot_resid = pl.BlockSpec((1, half, width), lambda i, core: (0, 0, 0))
    return pl.pallas_call(
        functools.partial(local_backward_body, nb, na),
        out_shape=[jax.ShapeDtypeStruct(shape, kind) for shape, kind in outs],
        grid_spec=pltpu.PrefetchScalarGridSpec(
            num_scalar_prefetch=1,
            grid=(1,),
            in_specs=[
                pl.BlockSpec((entries, half, width), lambda i, core: (0, core[0], 0)),
                pl.BlockSpec((half, width), lambda i, core: (core[0], 0)),
                whole_spec(vecs.shape),
                whole_spec(mix_in.shape),
                whole_spec(mix_out.shape),
                whole_spec(weights.shape),
                whole_spec(pre.shape),
                slot,
                slot,
                whole_spec(moved_first.shape),
                whole_spec(moved_last.shape),
                slot_resid,
                slot_resid,
                whole_spec(moved_resid.shape),
                whole_spec(bias_rows.shape),
            ],
            out_specs=[whole_spec(shape) for shape, _ in outs],
            scratch_shapes=[
                pltpu.VMEM((half, width), BF16),
                pltpu.VMEM((half, LANES), BF16),
                pltpu.VMEM((half, width), F32),
                pltpu.VMEM((8, width), F32),
                pltpu.VMEM((misc_rows, LANES), F32),
            ],
        ),
        cost_estimate=pl.CostEstimate(flops=150_000_000, bytes_accessed=12_000_000, transcendentals=0),
        name="local_backward",
    )(
        core, history, cotangent, vecs, mix_in, mix_out, weights, pre, own, got, moved_first, moved_last, own_resid,
        got_resid, moved_resid, bias_rows,
    )


SENT_FIRST = {(1, 0): (0, 0), (3, 0): (0, 1), (2, 1): (1, 0), (3, 1): (1, 1)}
KEPT = {(0, 0): 2, (2, 0): 3, (0, 1): 4, (1, 1): 5}


def piece_of(refs, index):
    if len(refs) == 1:
        return refs[0]
    piece = divmod(index, 2)
    if piece in KEPT:
        return refs[KEPT[piece]]
    which, place = SENT_FIRST[piece]
    return refs[which].at[place]


def piece_outs(shape, square):
    return [(2, *shape)] * 2 + [shape] * 4 if square else [shape]


def block_starts(info, nb, na, width, relative, square):
    size = width // (nb * na)
    if size % LANES:
        return [i * LANES for i in range(width // LANES)], LANES
    starts = []
    for slot in range(na):
        row = lax.bitwise_xor(info[1], slot) if relative and square else slot
        for step in range(nb):
            line = info[2] - step
            line = jnp.where(line < 0, line + nb, line)
            starts.append(pl.multiple_of((row * nb + line) * size, size))
    return starts, size


def feed_forward_body(nb, na, square, info, *refs):
    x_slots, g_slots, refs = refs[: 2 * nb], refs[2 * nb : 4 * nb], refs[4 * nb :]
    count = 2 * na if square else 1
    ups, downs, bias, refs = refs[:count], refs[count : 2 * count], refs[2 * count], refs[2 * count + 1 :]
    count = 6 if square else 1
    grads_up, grads_down, refs = refs[:count], refs[count : 2 * count], refs[2 * count :]
    grad_bias, part_own, part_other, branch_own, branch_other = refs[:5]
    x_all, g_all, x_turned, part_sum, branch_sum = refs[5:]
    step = pl.program_id(0)
    half, width = x_slots[0].shape
    rows = nb * half
    starts, size = block_starts(info, nb, na, width, True, square)

    @pl.when(step == 0)
    def _():
        for i, start in enumerate(starts):
            at, lanes = slice(i * size, (i + 1) * size), pl.ds(start, size)
            for slot in range(2 * nb):
                mine = slice(slot * half, (slot + 1) * half)
                x_all[mine, at] = x_slots[slot][:, lanes]
                g_all[mine, at] = g_slots[slot][:, lanes]
            x_turned[at, :] = x_all[:, at].T

    up = jnp.concatenate([piece[...] for piece in ups], 0)
    up_pre = mm(x_all[...], up) + bias[...]
    cdf, pdf = phi_parts(up_pre)
    gelu_out = (up_pre * cdf).astype(BF16)
    wide = jnp.concatenate([piece[i] for piece in downs for i in range(piece.shape[0])], -1)
    grad_gelu = mm(g_all[...], wide, NT)
    grad_up = (grad_gelu * (cdf + up_pre * pdf)).astype(BF16)
    grad_bias[...] = jnp.sum(grad_up.astype(F32), 0, keepdims=True)
    grad = mm(x_turned[...], grad_up).astype(BF16)
    each = ups[0].shape[0]
    for index in range(len(ups)):
        piece_of(grads_up, index)[...] = grad[index * each : (index + 1) * each]
    grad = mm(gelu_out.T, g_all[...]).astype(BF16)
    each, _, lanes = downs[0].shape
    for index in range(len(downs)):
        piece = piece_of(grads_down, index)
        for i in range(each):
            at = (index * each + i) * lanes
            piece[i] = grad[:, at : at + lanes]
    part = mm(grad_up, up, NT)
    branch = mm(gelu_out, wide)

    @pl.when(step == 0)
    def _():
        part_sum[...] = part
        branch_sum[...] = branch

    @pl.when(step > 0)
    def _():
        part_sum[...] += part
        branch_sum[...] += branch

    @pl.when(step == pl.num_programs(0) - 1)
    def _():
        for i, start in enumerate(starts):
            at, lanes = slice(i * size, (i + 1) * size), pl.ds(start, size)
            part_own[:, lanes] = part_sum[:rows, at]
            part_other[:, lanes] = part_sum[rows:, at].astype(BF16)
            branch_own[:, lanes] = branch_sum[:rows, at]
            branch_other[:, lanes] = branch_sum[rows:, at]


def feed_forward(info, x_slots, g_slots, ups, downs, bias, nb, na, square):
    half, width = x_slots[0].shape
    rows = nb * half
    hidden = bias.shape[1]
    tile = 256

    def tiled(shape):
        dim = max(i for i, size in enumerate(shape) if size == hidden)
        block = tuple(tile if i == dim else size for i, size in enumerate(shape))
        return pl.BlockSpec(block, lambda j, info: tuple(j if i == dim else 0 for i in range(len(shape))))

    fixed = pl.BlockSpec((rows, width), lambda j, info: (0, 0), pipeline_mode=pl.Buffered(1))
    outs = [(shape, BF16, tiled(shape)) for shape in piece_outs(ups[0].shape, square)]
    outs += [(shape, BF16, tiled(shape)) for shape in piece_outs(downs[0].shape, square)]
    outs += [
        ((1, hidden), F32, tiled((1, hidden))),
        ((rows, width), F32, fixed),
        ((rows, width), BF16, fixed),
        ((rows, width), F32, fixed),
        ((rows, width), F32, fixed),
    ]
    results = pl.pallas_call(
        functools.partial(feed_forward_body, nb, na, square),
        out_shape=[jax.ShapeDtypeStruct(shape, kind) for shape, kind, _ in outs],
        grid_spec=pltpu.PrefetchScalarGridSpec(
            num_scalar_prefetch=1,
            grid=(hidden // tile,),
            in_specs=[pl.BlockSpec((half, width), lambda j, info: (0, 0), pipeline_mode=pl.Buffered(1))] * (4 * nb)
            + [tiled(value.shape) for value in (*ups, *downs, bias)],
            out_specs=[spec for _, _, spec in outs],
            scratch_shapes=[
                pltpu.VMEM((2 * rows, width), BF16),
                pltpu.VMEM((2 * rows, width), BF16),
                pltpu.VMEM((width, 2 * rows), BF16),
                pltpu.VMEM((2 * rows, width), F32),
                pltpu.VMEM((2 * rows, width), F32),
            ],
        ),
        compiler_params=pltpu.CompilerParams(vmem_limit_bytes=60 * 1024 * 1024),
        cost_estimate=pl.CostEstimate(
            flops=24 * rows * width * hidden, bytes_accessed=32_000_000, transcendentals=4 * rows * hidden
        ),
        name="feed_forward",
    )(info, *x_slots, *g_slots, *ups, *downs, bias)
    count = 6 if square else 1
    return results[:count], results[count : 2 * count], *results[2 * count :]


def rotary_tables(length):
    half_rot = ROT // 2
    frequency = np.exp(np.arange(half_rot) * (-2.0 * math.log(10000.0) / ROT))
    angles = np.arange(length)[:, None] * frequency[None, :]
    tables = np.zeros((3, length, HEAD_DIM), np.float32)
    tables[0] = 1.0
    tables[0, :, :half_rot] = tables[0, :, half_rot:ROT] = np.cos(angles)
    tables[1, :, half_rot:ROT] = np.sin(angles)
    tables[2, :, :half_rot] = -np.sin(angles)
    return tables


def turn(values, cosine, rising, falling):
    half_rot = ROT // 2
    return (
        values * cosine
        + pltpu.roll(values, half_rot, 1) * rising
        + pltpu.roll(values, HEAD_DIM - half_rot, 1) * falling
    )


def attention_body(seqs, na, square, info, *refs):
    x_slots, g_slots, refs = refs[: 2 * seqs], refs[2 * seqs : 4 * seqs], refs[4 * seqs :]
    count = 2 * na if square else 1
    pieces, refs = refs[:count], refs[count:]
    bias, tables, branch_own, branch_other = refs[:4]
    count = 6 if square else 1
    grads, refs = refs[4 : 4 + count], refs[4 + count :]
    grad_bias, own = refs[:2]
    others, refs = refs[2 : 2 + seqs], refs[2 + seqs :]
    pre, table, mixed, grad_mixed, grad_pre, x_turned, out_w, weights, g_turned, x_all, g_all = refs
    core = info
    _, half, width = x_slots[0].shape
    starts, size = block_starts(info, seqs, na, width, True, square)
    part_rows = pieces[0].shape[0]
    per = part_rows // size
    for i, start in enumerate(starts):
        weights[pl.ds(start, size), :] = pieces[i // per][i % per * size : (i % per + 1) * size, :]

    def store_grad(row, lanes, value):
        at = slice(row % part_rows, row % part_rows + value.shape[0])
        piece_of(grads, row // part_rows)[at, lanes] = value.astype(BF16)

    length = 2 * half
    cols = bias.shape[1] // 3
    heads = cols // HEAD_DIM
    blocks = weights.shape[0] // LANES
    first = pl.multiple_of(core[0] * half, half)
    second = pl.multiple_of((1 - core[0]) * half, half)
    for kind in range(3):
        table[kind, :half] = tables[kind, pl.ds(first, half), :]
        table[kind, half:] = tables[kind, pl.ds(second, half), :]

    for slot in range(2 * seqs):
        at = slot % seqs * length + slot // seqs * half
        x_all[:, at : at + half, :] = x_slots[slot][...]
        g_all[at : at + half, :] = g_slots[slot][...]
    for kind in range(3):
        lanes = slice(kind * cols, (kind + 1) * cols)
        pre[kind] = mm(x_all[kind], weights[:, lanes]) + bias[:, lanes]

    for i in range(blocks):
        for part in range(cols // LANES):
            at = 3 * cols + part * LANES
            out_w[part * LANES : (part + 1) * LANES, i * LANES : (i + 1) * LANES] = weights[
                i * LANES : (i + 1) * LANES, at : at + LANES
            ]
    grad_mixed[0] = mm(g_all[...], out_w[...], NT)

    scale = HEAD_DIM ** (-0.5)
    row = lax.broadcasted_iota(jnp.int32, (length, length), 0)
    col = lax.broadcasted_iota(jnp.int32, (length, length), 1)
    row_at = jnp.where(row < half, row + core[0] * half, row - core[0] * half)
    col_at = jnp.where(col < half, col + core[0] * half, col - core[0] * half)
    causal = row_at >= col_at

    def one_seq(seq, _):
        at = pl.ds(pl.multiple_of(seq * length, length), length)
        cosine, rising, falling = table[0], table[1], table[2]
        for head in range(heads):
            lanes = slice(head * HEAD_DIM, (head + 1) * HEAD_DIM)
            query = turn(pre[0, at, lanes], cosine, rising, falling).astype(BF16)
            key = turn(pre[1, at, lanes], cosine, rising, falling).astype(BF16)
            value = pre[2, at, lanes].astype(BF16)
            scores = jnp.where(causal, mm(query, key, NT) * scale, -1e30)
            expon = jnp.exp(scores - jnp.max(scores, -1, keepdims=True))
            probs = expon / jnp.sum(expon, -1, keepdims=True)
            low = probs.astype(BF16)
            mixed[at, lanes] = mm(low, value).astype(BF16)
            grad = grad_mixed[0, at, lanes].astype(BF16)
            grad_value = mm(low, grad, TN)
            grad_probs = mm(grad, value, NT)
            delta = jnp.sum(probs * grad_probs, -1, keepdims=True)
            grad_scores = (probs * (grad_probs - delta)).astype(BF16)
            grad_query = mm(grad_scores, key) * scale
            grad_key = mm(grad_scores, query, TN) * scale
            grad_pre[0, at, lanes] = turn(grad_query, cosine, -rising, -falling).astype(BF16)
            grad_pre[1, at, lanes] = turn(grad_key, cosine, -rising, -falling).astype(BF16)
            grad_pre[2, at, lanes] = grad_value.astype(BF16)
        return 0

    lax.fori_loop(0, seqs, one_seq, 0)

    for i in range(blocks):
        g_turned[:, i * LANES : (i + 1) * LANES] = g_all[:, pl.ds(starts[i], LANES)]
    mixed_all = mixed[...]
    for seq in range(seqs):
        at, mid = seq * length, seq * length + half
        rows_own = slice(seq * half, (seq + 1) * half)
        own[seq, 0] = branch_own[rows_own] + mm(mixed_all[at:mid], out_w[...])
        others[seq][0] = (branch_other[rows_own] + mm(mixed_all[mid : mid + half], out_w[...])).astype(BF16)
    grad_out = mm(mixed_all.T, g_turned[...])
    for i in range(blocks):
        for part in range(cols // LANES):
            at = 3 * cols + part * LANES
            store_grad(
                i * LANES,
                slice(at, at + LANES),
                grad_out[part * LANES : (part + 1) * LANES, i * LANES : (i + 1) * LANES],
            )
    for kind in range(3):
        grad = grad_pre[kind]
        grad_bias[:, kind * cols : (kind + 1) * cols] = jnp.sum(grad.astype(F32), 0, keepdims=True)
        for i in range(blocks):
            x_turned[i * LANES : (i + 1) * LANES, :] = x_all[kind, :, pl.ds(starts[i], LANES)].T
        for start in range(0, width, part_rows):
            store_grad(
                start,
                slice(kind * cols, (kind + 1) * cols),
                mm(x_turned[start : start + part_rows, :], grad),
            )
        part = mm(grad, weights[:, kind * cols : (kind + 1) * cols], NT)
        for seq in range(seqs):
            at, mid = seq * length, seq * length + half
            own[seq, kind + 1] = part[at:mid]
            others[seq][kind + 1] = part[mid : mid + half].astype(BF16)


def attention(info, x_slots, g_slots, pieces, bias, tables, branch_own, branch_other, seqs, na, square):
    _, half, width = x_slots[0].shape
    rows = seqs * half
    cols = bias.shape[1] // 3
    piece = pieces[0].shape
    outs = [(shape, BF16) for shape in piece_outs(piece, square)]
    outs += [(bias.shape, F32), ((seqs, 4, half, width), F32)]
    outs += [((4, half, width), BF16)] * seqs
    operands = (*x_slots, *g_slots, *pieces, bias, tables, branch_own, branch_other)
    one = lambda shape: pl.BlockSpec(shape, lambda *_: (0,) * len(shape), pipeline_mode=pl.Buffered(1))
    return pl.pallas_call(
        functools.partial(attention_body, seqs, na, square),
        out_shape=[jax.ShapeDtypeStruct(shape, kind) for shape, kind in outs],
        grid_spec=pltpu.PrefetchScalarGridSpec(
            num_scalar_prefetch=1,
            grid=(1,),
            in_specs=[one(value.shape) for value in operands],
            out_specs=[one(shape) for shape, _ in outs],
            scratch_shapes=[
                pltpu.VMEM((3, 2 * rows, cols), F32),
                pltpu.VMEM((3, 2 * half, HEAD_DIM), F32),
                pltpu.VMEM((2 * rows, cols), BF16),
                pltpu.VMEM((1, 2 * rows, cols), F32),
                pltpu.VMEM((3, 2 * rows, cols), BF16),
                pltpu.VMEM((width, 2 * rows), BF16),
                pltpu.VMEM((cols, width), BF16),
                pltpu.VMEM((width, piece[1]), BF16),
                pltpu.VMEM((2 * rows, width), BF16),
                pltpu.VMEM((3, 2 * rows, width), BF16),
                pltpu.VMEM((2 * rows, width), BF16),
            ],
        ),
        compiler_params=pltpu.CompilerParams(vmem_limit_bytes=62 * 1024 * 1024),
        cost_estimate=pl.CostEstimate(
            flops=48 * rows * width * cols, bytes_accessed=32_000_000, transcendentals=rows * cols
        ),
        name="attention",
    )(info, *operands)


def after(value, *needed):
    return lax.optimization_barrier((value, needed))[0]


def ring(values):
    return shift_b(values, 1)


def swap_core(values):
    return lax.ppermute(values, "mp", SWAP)


def shift_b(values, step):
    size = lax.axis_size("b")
    return lax.ppermute(values, "b", [(i, (i + step) % size) for i in range(size)])


def exchange_b(block_of):
    nb, line = lax.axis_size("b"), lax.axis_index("b")
    slots = [block_of(lax.rem(line + step, nb)) for step in range(nb)]
    return [shift_b(block, step) if step else block for step, block in enumerate(slots)]


def by_line(slots):
    nb, line = lax.axis_size("b"), lax.axis_index("b")
    blocks = jnp.stack(slots)
    return [lax.dynamic_index_in_dim(blocks, lax.rem(line - i + nb, nb), 0, keepdims=False) for i in range(nb)]


def gather_a(blocks):
    return lax.all_gather(blocks, "a", axis=0, tiled=True)


def across(values, bits):
    return lax.ppermute(values, "a", [(i, i ^ bits) for i in range(lax.axis_size("a"))])


def gather_square(slots):
    middle = len(slots) // 2
    first, second = jnp.concatenate(slots[:middle]), jnp.concatenate(slots[middle:])
    first_x, second_y = across(first, 1), across(second, 2)
    first_y, second_x = across(first, 2), across(second, 1)
    first_xy, second_xy = across(first_x, 2), across(second_y, 1)
    return [first, second, first_x, second_x, first_y, second_y, first_xy, second_xy]


def scatter_square(grads, nb, needed=()):
    sent_x, sent_y, first, first_y, second, second_x = grads
    got_x, got_y = across(sent_x, 1), across(sent_y, 2)
    add = lambda left, right: left.astype(F32) + right.astype(F32)
    first_y = add(first_y, got_x[1]).astype(BF16)
    second_x = add(second_x, got_y[1]).astype(BF16)
    first_y, second_x = across(first_y, 2), across(second_x, 1)
    first_y, second_x = after((first_y, second_x), needed)
    blocks = []
    per = nb // 2
    each = first.shape[0] // per
    for kept, got, last in ((first, got_x[0], first_y), (second, got_y[0], second_x)):
        for i in range(per):
            at = slice(i * each, (i + 1) * each)
            blocks.append(add(kept[at], got[at]) + last[at].astype(F32))
    return blocks


def scatter_a(grad):
    return lax.psum_scatter(grad, "a", scatter_dimension=0, tiled=True)


def grads_home(mine):
    nb = lax.axis_size("b")
    return [shift_b(mine[step].astype(BF16), -step) if step else mine[0] for step in range(nb)]


def place(slots, axis):
    nb = len(slots)
    line = lax.axis_index("b")
    size = slots[0].shape[axis]
    shape = list(slots[0].shape)
    shape[axis] *= nb
    out = jnp.zeros(shape, F32)
    for step, slot in enumerate(slots):
        at = lax.rem(line + step, nb) * size
        out = lax.dynamic_update_slice_in_dim(out, slot.astype(F32), at, axis)
    return out


def place_vector(values, full_len, index):
    return lax.dynamic_update_slice_in_dim(
        jnp.zeros((full_len,), F32), values, index * values.shape[0], 0
    )


def sum_small(small):
    tiles = small.shape[1]
    dp = ("b", "a")
    mine = small[0] + swap_core(small[1])
    if lax.axis_size(dp) == tiles:
        blocks = lax.all_to_all(mine, dp, 0, 0, tiled=True)
        mine = lax.all_to_all(jnp.broadcast_to(jnp.sum(blocks, 0), mine.shape), dp, 0, 0, tiled=True)
    else:
        mine = lax.psum(mine, dp)
    other = swap_core(mine)
    first = lax.axis_index("mp") == 0
    return jnp.concatenate([jnp.where(first, mine, other), jnp.where(first, other, mine)], 1)


def shards(
    history, cotangent, weight_query, weight_key, weight_value, weight_out, weight_up, weight_down,
    bias_query, bias_key, bias_value, out_bias, bias_up, attn_gain, attn_shift, mlp_gain, mlp_shift,
    mix_gain, mix_in, mix_out, mix_bias,
):
    _, length, width = history.shape
    nb, na, n_mp = lax.axis_size("b"), lax.axis_size("a"), lax.axis_size("mp")
    line, core = lax.axis_index("b"), lax.axis_index("mp")
    half = length // n_mp
    own_rows = width // (nb * na)
    mix_hid = mix_in.shape[1]
    core_ref = jnp.stack([core, lax.axis_index("a"), line]).astype(jnp.int32)
    square = na == 4

    hidden = weight_up.shape[1] // nb
    up_slots = exchange_b(lambda i: lax.dynamic_slice_in_dim(weight_up, i * hidden, hidden, 1))
    whole_lanes = own_rows % LANES == 0
    line_order = (lambda slots: slots) if whole_lanes else by_line
    if square:
        full_up = gather_square(up_slots)
    else:
        full_up = [gather_a(jnp.stack(line_order(up_slots))).reshape(width, -1)]

    vecs = jnp.stack([attn_gain, attn_shift, mlp_gain, mlp_shift, mix_gain, out_bias]).astype(F32)
    mix_in_t = jnp.pad(mix_in.T, ((0, LANES - mix_hid), (0, 0)))
    mix_out_p = jnp.pad(mix_out, ((0, LANES - mix_hid), (0, LANES - mix_out.shape[1])))
    mix_bias_p = jnp.pad(mix_bias.astype(F32), (0, LANES - mix_bias.shape[0])).reshape(1, LANES)
    in_qkv, in_resid, cot, mix_weights, mix_pre = local_forward(
        core_ref, history, cotangent, vecs, mix_in_t, mix_out_p, mix_bias_p, nb, na, half
    )

    down = weight_down
    down_slots = exchange_b(lambda i: lax.dynamic_slice_in_dim(down, i * hidden, hidden, 0))
    if square:
        full_down = gather_square([slot[None] for slot in down_slots])
    else:
        full_down = [gather_a(jnp.stack(line_order(down_slots)))]

    def gather_tokens(values):
        slots = [values]
        for _ in range(1, nb):
            slots.append(ring(slots[-1]))
        return [*slots, *(swap_core(slot) for slot in slots)]

    g_slots = gather_tokens(cot)
    x_slots = gather_tokens(in_resid)
    qkv_slots = gather_tokens(in_qkv)

    bias_up_mine = lax.dynamic_slice_in_dim(bias_up, line * hidden, hidden, 0).astype(F32)
    grad_up, grad_down, grad_bias_up, part_own, part_other, branch_own, branch_other = feed_forward(
        core_ref, x_slots, g_slots, full_up, full_down, bias_up_mine.reshape(1, -1), nb, na, square
    )

    def scatter_tokens(mine, theirs):
        moving = mine[1] + theirs[1].astype(F32)
        for step in range(2, nb):
            arrived = ring(moving.astype(BF16))
            moving = arrived.astype(F32) + (mine[step] + theirs[step].astype(F32))
        return ring(moving.astype(BF16)), arrived

    def send_home(mine, theirs):
        moved = []
        for step in range(1, nb):
            pair = (mine[step] + theirs[step].astype(F32)).astype(BF16)
            moved.append(shift_b(pair, -step).astype(F32))
        return sum(moved[1:], moved[0])

    part_own = part_own.reshape(nb, half, width)
    got_resid = swap_core(part_other.reshape(nb, half, width))
    moved_resid = send_home(part_own, got_resid)
    head_cols = weight_query.shape[1] // nb
    groups = head_cols // HEAD_DIM
    pieces = [w.reshape(own_rows, nb, head_cols).transpose(1, 0, 2) for w in (weight_query, weight_key, weight_value)]
    out_blocks = weight_out.reshape(nb, groups, HEAD_DIM, own_rows)
    packed = own_rows == LANES
    if not packed:
        out_blocks = weight_out.reshape(nb, head_cols, own_rows).transpose(0, 2, 1)
        pieces.append(out_blocks)
    else:
        pieces.extend(out_blocks[:, group] for group in range(groups))
    attn_blocks = jnp.concatenate(pieces, -1)
    attn_slots = exchange_b(lambda i: lax.dynamic_index_in_dim(attn_blocks, i, 0, keepdims=False))
    attn_slots = after(attn_slots, grad_bias_up)
    if square:
        full_attn = gather_square(attn_slots)
    else:
        full_attn = [gather_a(jnp.stack(line_order(attn_slots))).reshape(width, -1)]
    biases = [
        lax.dynamic_slice_in_dim(bias, line * head_cols, head_cols, 0).astype(F32)
        for bias in (bias_query, bias_key, bias_value)
    ]
    if not packed:
        full_attn = [repack_out(full_attn[0], head_cols, True)]
    results = attention(
        core_ref, qkv_slots, g_slots, full_attn, jnp.concatenate(biases).reshape(1, -1),
        jnp.asarray(rotary_tables(length)), branch_own, branch_other, nb, na, square,
    )
    other = results[-nb:]
    *grad_attn, grad_bias_attn, own = results[:-nb]

    got = {slot: swap_core(other[slot]) for slot in (*range(1, nb), 0)}
    moved_first, _ = scatter_tokens(own[:, :2], {slot: got[slot][:2] for slot in got})
    moved_last, arrived = scatter_tokens(own[:, 2:], {slot: got[slot][2:] for slot in got})

    block = core * nb + line
    tiles = width // LANES
    rows_of = lambda value, full: place_vector(value, full, block).reshape(-1, tiles, LANES).transpose(1, 0, 2)
    bias_rows = [rows_of(grad_bias_up.reshape(-1), bias_up.shape[0] * n_mp)]
    for kind in range(3):
        bias_rows.append(rows_of(grad_bias_attn[0, kind * head_cols : (kind + 1) * head_cols], width))
    bias_rows = jnp.concatenate(bias_rows, 1)
    bias_count = bias_rows.shape[1]
    bias_rows = jnp.pad(bias_rows, ((0, 0), (0, -bias_count % 16 if bias_count % 16 > 8 else -bias_count % 8), (0, 0)))

    grad_history, block_half, small = local_backward(
        core_ref, history, cotangent, vecs, mix_in_t, mix_out_p, mix_weights, mix_pre, own, got[0][None], moved_first, moved_last,
        part_own, got_resid, moved_resid, bias_rows, nb, na, half,
    )
    block_other = swap_core(block_half)
    first = core == 0
    block_out = jnp.concatenate(
        [jnp.where(first, block_half, block_other), jnp.where(first, block_other, block_half)], 0
    )
    small = sum_small(small)

    if square:
        up_sum = scatter_square(grad_up, nb, arrived)
        down_sum = [block.reshape(-1, own_rows) for block in scatter_square(grad_down, nb, arrived)]
        attn_sum = scatter_square(grad_attn, nb)
    else:
        up_sum = scatter_a(grad_up[0].reshape(na * nb, own_rows, -1))
        down_sum = scatter_a(grad_down[0])
        grad_attn = grad_attn[0]
        if not packed:
            grad_attn = repack_out(grad_attn, head_cols, False)
        attn_sum = scatter_a(grad_attn.reshape(na * nb, own_rows, -1))
        up_sum, down_sum, attn_sum = (line_order(value) for value in (up_sum, down_sum, attn_sum))
    up_slots, down_slots = grads_home(up_sum), grads_home(down_sum)
    up_shard, down_shard = place(up_slots, 1), place(down_slots, 0)
    attn_slots = grads_home(attn_sum)
    shards_qkv = [
        place([slot[:, kind * head_cols : (kind + 1) * head_cols] for slot in attn_slots], 1)
        for kind in range(3)
    ]
    if packed:
        out_slots = [
            jnp.concatenate(
                [slot[:, 3 * head_cols + g * LANES : 3 * head_cols + (g + 1) * LANES] for g in range(groups)], 0
            )
            for slot in attn_slots
        ]
    else:
        out_slots = [slot[:, 3 * head_cols :].T for slot in attn_slots]
    out_shard = place(out_slots, 0)

    line_of = lambda row: small[:, row, :].reshape(-1)
    misc = small[:, 80:88, :].reshape(-1, LANES)
    tokens = length * nb * na
    n_mix = mix_bias.shape[0]
    mean_weights = misc[73, :n_mix] / tokens
    var_weights = misc[74, :n_mix] / tokens - mean_weights * mean_weights
    up_rows = bias_up.shape[0] * n_mp // width
    biases = small[:, 88 : 88 + bias_count, :].transpose(1, 0, 2).reshape(bias_count, width)
    return (
        block_out,
        grad_history,
        *shards_qkv,
        out_shard,
        up_shard,
        down_shard,
        biases[up_rows],
        biases[up_rows + 1],
        biases[up_rows + 2],
        line_of(77),
        biases[:up_rows].reshape(-1),
        line_of(72),
        line_of(73),
        line_of(74),
        line_of(75),
        line_of(76),
        small[:, :mix_hid, :].transpose(1, 0, 2).reshape(mix_hid, width).T,
        misc[:mix_hid, :n_mix],
        misc[72, :n_mix],
        jnp.stack([mean_weights, var_weights]),
    )


def repack_out(weights, cols, forward):
    width = weights.shape[0]
    lead, part = weights[:, : 3 * cols], weights[:, 3 * cols :]
    part = part.reshape(width // LANES, LANES, cols // LANES, LANES).transpose(0, 3, 2, 1)
    del forward
    return jnp.concatenate([lead, part.reshape(width, cols)], 1)


def solution(mesh):
    n_dp, n_mp = mesh.shape["dp"], mesh.shape["mp"]
    fine = Mesh(mesh.devices.reshape(NB, n_dp // NB, n_mp), ("b", "a", "mp"))
    dp = ("b", "a")
    whole = P()
    in_specs = (
        P(None, dp, None),
        P(dp, None),
        P(dp, "mp"),
        P(dp, "mp"),
        P(dp, "mp"),
        P("mp", dp),
        P(dp, "mp"),
        P("mp", dp),
        P("mp"),
        P("mp"),
        P("mp"),
        whole,
        P("mp"),
    ) + (whole,) * 8
    out_specs = (
        P(dp, None),
        P(None, dp + ("mp",), None),
        P(dp, "mp"),
        P(dp, "mp"),
        P(dp, "mp"),
        P("mp", dp),
        P(dp, "mp"),
        P("mp", dp),
    ) + (whole,) * 14
    return jax.shard_map(shards, mesh=fine, in_specs=in_specs, out_specs=out_specs, check_vma=False)
```
